512 devices in a mesh: wall: 32 (over y, x, core), stream: 16 (over z).
Axes of the slice: x: 4, y: 4, z: 16, core: 2. Of those that a mesh axis runs over, the one named last changes fastest.
Arguments:
- cotangent: float32 [5, 16, 1024, 4096], P(None, None, 'wall', 'stream'), may hold values from -6 to 6
- lower: float32 [5, 1024], P(None, 'wall'), may hold values from 0 to 1, as said below
- pivot: float32 [5, 1024], P(None, 'wall'), as said below
- speed: float32 [5, 1024], P(None, 'wall'), may hold values from 0.5 to 2
Outputs:
- state_grad: float32 [5, 16, 1024, 4096], P(None, None, 'wall', 'stream')
The draws below stay inside these ranges and needn't reach their ends.
Inputs may be any that keep to these rules, and one draw needn't show every extreme that they name: `lower`: every multiplier is strictly between 0 and 1. Every pivot is positive.
All inputs are finite; a program needn't handle non-finite values.
Results may differ from the reference program's by a relative error of at most 0.00012.
Values sent between devices are 32-bit elements; how exact they have to be, the bound alone decides.
No kernel may reach another device: no remote copies, remote signals or barrier semaphores. Data moves between devices by JAX's collectives and lax.ppermute only.
A program may use at most 64 MiB of HBM per device.

```python
import math
import jax
import jax.numpy as jnp
from jax import lax

FLOW_VARIABLES = 5
PLANES = 16
CY = 32
NORMAL_ROWS = 1024
NX = 4096


def decay_pair(key):
    parent_key = jax.random.fold_in(key, 17)
    sluggish_key, row_key, block_key, spike_key, trim_key = jax.random.split(parent_key, 5)
    slow_mask = jax.random.uniform(sluggish_key, (FLOW_VARIABLES,)) < 0.5
    base_rate = jnp.where(slow_mask, 0.15 / NORMAL_ROWS, 0.02)
    row_factor = jnp.exp(jax.random.uniform(row_key, (FLOW_VARIABLES, NORMAL_ROWS), minval=math.log(0.3), maxval=math.log(3.0)))
    block_factor = jnp.exp(jax.random.uniform(block_key, (FLOW_VARIABLES, NORMAL_ROWS // CY), minval=math.log(0.5), maxval=math.log(2.0)))
    rate_all = base_rate[:, None] * row_factor * jnp.repeat(block_factor, CY, axis=1)
    retain_rate = jnp.exp(-rate_all)
    spike_rows = jax.random.randint(spike_key, (FLOW_VARIABLES, 2), 0, NORMAL_ROWS)
    location_list = jnp.arange(NORMAL_ROWS)
    spike_mask = jnp.any(location_list[None, :, None] == spike_rows[:, None, :], axis=2)
    trim_factor = jax.random.uniform(trim_key, (FLOW_VARIABLES, NORMAL_ROWS), minval=0.5, maxval=0.8)
    retain_rate = jnp.where(spike_mask, retain_rate * trim_factor, retain_rate)
    return (retain_rate, base_rate)


def draw_lower(key, part):
    retain_rate, base_rate = decay_pair(key)
    return retain_rate.astype(jnp.float32)


def draw_pivot(key, part):
    retain_rate, base_rate = decay_pair(key)
    rough = jnp.exp(jax.random.uniform(jax.random.fold_in(key, 29), (FLOW_VARIABLES, NORMAL_ROWS), minval=math.log(0.5), maxval=math.log(2.0)))
    scale_field = 0.5 * (1.27 * base_rate + math.pi / NORMAL_ROWS) ** (-1.5)
    return (scale_field[:, None] * rough).astype(jnp.float32)


def block_scale(stream_key, extent, cuts, low, top_value):
    gain = 1.0
    for axis_at, shards_of in cuts:
        steps = jax.random.uniform(jax.random.fold_in(jax.random.fold_in(stream_key, 6), axis_at), (shards_of,), jnp.float32, low / len(cuts), top_value / len(cuts))
        gain = gain * jnp.repeat(jnp.exp(steps), extent[axis_at] // shards_of).reshape((-1,) + (1,) * (len(extent) - 1 - axis_at))
    return gain


def scatter_about(rng, extent, width, bound, pieces=(), kind=jnp.bfloat16):
    drawn = jax.random.normal(rng, extent, jnp.float32) * width
    if len(pieces) > 0:
        drawn = block_scale(rng, extent, pieces, -0.22, 0.18) * drawn
    return jnp.clip(drawn, min=-bound, max=bound).astype(kind)


def setup_inputs(seed: int = 0) -> dict:
    key_of = jax.random.split(jax.random.key(seed), 5)
    cotangent = scatter_about(key_of[0], (FLOW_VARIABLES, PLANES, NORMAL_ROWS, NX), 1.0, 6.0, ((2, 32), (3, 16)), jnp.float32)
    lower = draw_lower(jax.random.fold_in(key_of[4], 71), 0)
    pivot = draw_pivot(jax.random.fold_in(key_of[4], 71), 0)
    speed = jnp.clip(0.5 + 1.5 * jax.random.uniform(key_of[3], (FLOW_VARIABLES, NORMAL_ROWS), jnp.float32) ** block_scale(key_of[3], (FLOW_VARIABLES, NORMAL_ROWS), ((1, 32),), -0.2, 0.2), 0.5, 2.0)
    return dict(cotangent=cotangent, lower=lower, pivot=pivot, speed=speed)


first_coeff = 7.0 / 9.0
second_coeff = 1.0 / 36.0


def line_solve(operands):
    gradient, lower_line, pivot_line, speed_line = operands
    by_rows = jnp.moveaxis(gradient, 1, 0)
    zeros_plane = jnp.zeros(by_rows.shape[1:], by_rows.dtype)

    def up_step(carried_in, element):
        value, factor = element
        current = value + carried_in
        return factor * current, current

    _, rising = lax.scan(up_step, zeros_plane, (by_rows, lower_line))
    scaled = rising / pivot_line[:, None, None]

    def down_step(carried_in, element):
        value, factor = element
        current = value + factor * carried_in
        return current, current

    _, adjoint = lax.scan(down_step, zeros_plane, (scaled, lower_line), reverse=True)
    flux_line = speed_line[:, None, None] * adjoint
    spectrum = jnp.fft.rfft(flux_line, axis=-1)
    angles = 2.0 * math.pi * jnp.arange(NX // 2 + 1).astype(flux_line.dtype) / NX
    symbol = 2.0 * (first_coeff * jnp.sin(angles) + second_coeff * jnp.sin(2.0 * angles)) / (1.0 + (2.0 / 3.0) * jnp.cos(angles))
    derivative = jnp.fft.irfft(spectrum * (1j * symbol), n=NX, axis=-1).astype(adjoint.dtype)
    return jnp.moveaxis(adjoint + derivative, 0, 1)


def reference(cotangent, lower, pivot, speed):
    return lax.map(line_solve, (cotangent, lower, pivot, speed))
```

```python
import math

import jax
import jax.numpy as jnp
import ml_dtypes
import numpy as np
from jax import lax
from jax.experimental import pallas as pl
from jax.experimental.pallas import tpu as pltpu
from jax.sharding import PartitionSpec as P

F32, BF16 = jnp.float32, jnp.bfloat16
R = (math.sqrt(5.0) - 3.0) / 2.0
GAIN = 3.0 / math.sqrt(5.0)
C1 = 7.0 / 9.0
C2 = 1.0 / 36.0
FIELDS, PLANES, ROWS, CELLS, WALLS = 5, 16, 32, 256, 32


def split_np(w):
    w = np.asarray(w, np.float64)
    hi = w.astype(ml_dtypes.bfloat16)
    lo = (w - hi.astype(np.float64)).astype(ml_dtypes.bfloat16)
    return hi, lo


def tables():
    dec = lambda n: np.where(np.abs(n) % 2 == 0, 1.0, -1.0) * np.abs(R) ** np.abs(n)
    off = np.arange(CELLS)[:, None] - np.arange(CELLS)[None, :]
    tap = lambda o: GAIN * (C1 * (dec(o - 1) - dec(o + 1)) + C2 * (dec(o - 2) - dec(o + 2)))
    whi, wlo = split_np(tap(off))
    kappa = GAIN * (C1 * (1.0 / R - R) + C2 * (R**-2 - R**2))
    corr = tap(np.array(-1)) + kappa * R
    x = np.arange(CELLS)
    ext = np.zeros((4, CELLS))
    ext[0] = kappa * dec(CELLS - x)
    ext[1, CELLS - 1] = -corr
    ext[2] = -kappa * dec(x + 1)
    ext[3, 0] = corr
    ehi, elo = split_np(np.repeat(ext, PLANES, axis=0))
    zero = np.zeros_like(elo)
    stencil = np.concatenate([whi, whi, wlo, ehi, elo, ehi, zero], axis=0)
    edge = np.zeros((CELLS, 4))
    edge[:, 0] = dec(x)
    edge[0, 1] = 1.0
    edge[:, 2] = dec(CELLS - 1 - x)
    edge[CELLS - 1, 3] = 1.0
    edge = np.concatenate([np.repeat(edge, PLANES, axis=1), np.zeros((CELLS, 64))], axis=1)
    ghi, glo = split_np(edge)
    return stencil, np.concatenate([ghi, ghi, glo], axis=0)


def halves(x):
    hi = x.astype(BF16)
    return hi, (x - hi.astype(F32)).astype(BF16)


def lanes(shape):
    return lax.broadcasted_iota(jnp.int32, shape, len(shape) - 1)


def sublanes(shape):
    return lax.broadcasted_iota(jnp.int32, shape, len(shape) - 2)


def edge_kernel(c_ref, w_ref, left_ref, right_ref):
    w = w_ref[...]
    lane32, lane = lanes((ROWS, 128)) % 16, lanes((8, 128)) // 32
    for f in range(FIELDS):
        tiles = c_ref[f].reshape(PLANES * 4, 2, 8, 128)
        rows = [tiles[:, h].reshape(PLANES * ROWS, 128) for h in range(2)]
        hi, lo = halves(jnp.concatenate(rows, axis=1))
        sums = jnp.dot(jnp.concatenate([hi, lo, hi], axis=1), w, preferred_element_type=F32)
        own = sums[:ROWS]
        for p in range(1, PLANES):
            own = jnp.where(lane32 == p, sums[p * ROWS : (p + 1) * ROWS], own)
        left = own[:8]
        right = pltpu.roll(own[:8], 96, 1)
        for q in range(1, 4):
            part = own[8 * q : 8 * q + 8]
            left = jnp.where(lane == q, pltpu.roll(part, 32 * q, 1), left)
            right = jnp.where(lane == q, pltpu.roll(part, (32 * q + 96) % 128, 1) if q != 1 else part, right)
        left_ref[f] = left
        right_ref[f] = right


def row_of(j, h):
    return (j // 8) * 16 + h * 8 + j % 8


def load_row(ref, f, j):
    return jnp.concatenate([ref[f, pl.ds(row_of(j, h), PLANES, stride=64), :] for h in range(2)], 1)


def spread_rows(ref, out_ref):
    value = ref[...]
    for j in range(ROWS):
        out_ref[j * 8 : j * 8 + FIELDS, :] = jnp.broadcast_to(value[:, j : j + 1], (FIELDS, 128))


def sums_kernel(c_ref, lower_ref, pivot_ref, out_ref, rise_ref, fall_ref, unit_ref):
    low, piv = lower_ref[...], pivot_ref[...]
    wide = lambda v, j: jnp.broadcast_to(v[:, j : j + 1], (FIELDS, 128))
    entry = jnp.ones((FIELDS, 128), F32)
    entries, inverse, spread = [], [], jnp.zeros((FIELDS, 128), F32)
    for j in range(ROWS):
        inverse.append(1.0 / wide(piv, j))
        entries.append(entry)
        spread = spread + entry * entry * inverse[j]
        entry = entry * wide(low, j)
    leave, first = None, None
    for j in reversed(range(ROWS)):
        l = wide(low, j)
        leave = l if leave is None else l * leave
        first = entries[j] * inverse[j] if first is None else entries[j] * inverse[j] + l * first
        rise_ref[j * 8 : j * 8 + FIELDS, :] = leave
        fall_ref[j * 8 : j * 8 + FIELDS, :] = first
    unit_ref[0, :FIELDS, :] = entry
    unit_ref[1, :FIELDS, :] = spread
    for f in range(FIELDS):
        up = jnp.zeros((PLANES, CELLS), F32)
        down = jnp.zeros((PLANES, CELLS), F32)
        for j in range(ROWS):
            v = load_row(c_ref, f, j)
            a = rise_ref[pl.ds(j * 8 + f, 8, stride=0), :]
            b = fall_ref[pl.ds(j * 8 + f, 8, stride=0), :]
            a = jnp.concatenate([jnp.concatenate([a, a], 0)] * 2, 1)
            b = jnp.concatenate([jnp.concatenate([b, b], 0)] * 2, 1)
            up = up + a * v
            down = down + b * v
        for h in range(2):
            for q in range(2):
                base = (16 * q + h) * 16 + f
                out_ref[pl.ds(base, 8, stride=32), :] = up[8 * q : 8 * q + 8, 128 * h : 128 * h + 128]
                out_ref[pl.ds(base + 8, 8, stride=32), :] = down[8 * q : 8 * q + 8, 128 * h : 128 * h + 128]


def merge_kernel(main_ref, rise_ref, fall_ref, unit_ref, left_ref, right_ref, out_ref, ext_ref):
    lane = lanes((8, 128))
    ups, downs = [], []
    for f in range(FIELDS):
        up = jnp.zeros((8, 128), F32)
        down = jnp.zeros((8, 128), F32)
        from_left, from_right = left_ref[f], right_ref[f]
        for q in range(4):
            r = pltpu.roll(from_right, (128 - 32 * q) % 128, 1) if q else from_right
            l = pltpu.roll(from_left, (128 - 32 * q + 32) % 128, 1) if q != 1 else from_left
            v = jnp.where(lane < 32, r, l)
            v = jnp.where(lane < 64, v, pltpu.roll(v, 64, 1))
            ext_ref[f, 8 * q : 8 * q + 8, :] = v
            up = up + rise_ref[pl.ds(64 * q + f, 8, stride=8), :] * v
            down = down + fall_ref[pl.ds(64 * q + f, 8, stride=8), :] * v
        ups.append(jnp.sum(up, axis=0, keepdims=True))
        downs.append(jnp.sum(down, axis=0, keepdims=True))
    for f in range(FIELDS, 8):
        ext_ref[f] = jnp.zeros((ROWS, 128), F32)
    row = sublanes((FIELDS, 128))
    lane5 = lanes((FIELDS, 128))
    coef = jnp.where(lane5 == 64 + row, unit_ref[0, :FIELDS, :], 0.0)
    coef = jnp.where(lane5 == 72 + row, unit_ref[1, :FIELDS, :], coef)
    coef = jnp.sum(coef, axis=0, keepdims=True)
    lane1 = lanes((1, 128))
    sub = sublanes((8, 128))

    def pack(v, last):
        rows = [jnp.where(lane1 < 64, v[0], v[1]), jnp.where(lane1 < 64, v[2], v[3]), jnp.where(lane1 < 64, v[4], last)]
        return jnp.where(sub == 5, rows[0], jnp.where(sub == 6, rows[1], rows[2]))

    tail_up, tail_down = pack(ups, coef), pack(downs, jnp.zeros((1, 128), F32))
    for k in range(WALLS):
        out_ref[k, :8, :] = jnp.where(sub < 5, main_ref[16 * k : 16 * k + 8, :], tail_up)
        out_ref[k, 8:, :] = jnp.where(sub < 5, main_ref[16 * k + 8 : 16 * k + 16, :], tail_down)


def carry_kernel(in_ref, out_ref, through_ref, crest_ref):
    sub, lane = sublanes((8, 128)), lanes((8, 128))
    low_field = jnp.where(sub < 5, sub, 2 * (sub - 5))
    high_field = jnp.where(sub < 5, sub, jnp.where(sub < 7, 2 * (sub - 5) + 1, 4))

    def pick(row, at):
        lo = jnp.sum(jnp.where(lane == at + low_field, row, 0.0), axis=1, keepdims=True)
        hi = jnp.sum(jnp.where(lane == at + high_field, row, 0.0), axis=1, keepdims=True)
        return jnp.where(lane < 64, lo, hi)

    run = jnp.zeros((8, 128), F32)
    for d in range(WALLS):
        row = jnp.broadcast_to(in_ref[d, 7:8, :], (8, 128))
        through, spread = pick(row, 64), pick(row, 72)
        through_ref[d] = through
        out_ref[d, :8, :] = run
        crest_ref[d] = in_ref[d, 8:, :] + spread * run
        run = through * run + in_ref[d, :8, :]
    run = jnp.zeros((8, 128), F32)
    for d in reversed(range(WALLS)):
        out_ref[d, 8:, :] = run
        run = through_ref[d] * run + crest_ref[d]


def final_kernel(c_ref, ret_ref, lower_ref, pivot_ref, speed_ref, ext_ref, w_ref, o_ref, low_ref, inv_ref, sp_ref, fe_ref, sc_ref, lhs_ref, res_ref, sem):
    spread_rows(lower_ref, low_ref)
    spread_rows(speed_ref, sp_ref)
    value = 1.0 / pivot_ref[...]
    for j in range(ROWS):
        inv_ref[j * 8 : j * 8 + FIELDS, :] = jnp.broadcast_to(value[:, j : j + 1], (FIELDS, 128))
    sub, lane = sublanes((8, 128)), lanes((8, 128))

    def unpack(tile):
        turned = pltpu.roll(tile, 64, 1)
        a, b = jnp.where(lane < 64, tile, turned), jnp.where(lane < 64, turned, tile)
        rows = [a[5:6], b[5:6], a[6:7], b[6:7], a[7:8]]
        out = jnp.broadcast_to(rows[4], (8, 128))
        for f in range(4):
            out = jnp.where(sub == f, rows[f], out)
        return jnp.where(sub < FIELDS, out, 0.0)

    run = unpack(ret_ref[0:8, :])
    for j in range(ROWS):
        run = ext_ref[pl.ds(j, 8, stride=ROWS), :] + run
        fe_ref[j * 8 : j * 8 + 8, :] = run * inv_ref[j * 8 : j * 8 + 8, :]
        run = run * low_ref[j * 8 : j * 8 + 8, :]
    run = unpack(ret_ref[8:16, :])
    for j in reversed(range(ROWS)):
        run = fe_ref[j * 8 : j * 8 + 8, :] + low_ref[j * 8 : j * 8 + 8, :] * run
        fe_ref[j * 8 : j * 8 + 8, :] = run * sp_ref[j * 8 : j * 8 + 8, :]

    mine = lanes((PLANES, 128)) % 16 == sublanes((PLANES, 128))
    w = w_ref[...]

    def full(ref, j, f):
        v = ref[pl.ds(j * 8 + f, 8, stride=0), :]
        return jnp.concatenate([jnp.concatenate([v, v], 0)] * 2, 1)

    copies = []
    for f in range(FIELDS):
        slot = f % 2

        def carry(shift):
            parts = [
                [ret_ref[pl.ds((16 * q + h) * 16 + f + shift, 8, stride=32), :] for h in range(2)] for q in range(2)
            ]
            return jnp.concatenate([jnp.concatenate(p, 1) for p in parts], 0)

        run = carry(0)
        for j in range(ROWS):
            run = load_row(c_ref, f, j) + run
            sc_ref[slot, j * 16 : j * 16 + 16, :] = run * full(inv_ref, j, f)
            run = run * full(low_ref, j, f)
        run = carry(8)
        for j in reversed(range(ROWS)):
            run = sc_ref[slot, j * 16 : j * 16 + 16, :] + full(low_ref, j, f) * run
            sc_ref[slot, j * 16 : j * 16 + 16, :] = run
            hi, lo = halves(run * full(sp_ref, j, f))
            e = fe_ref[pl.ds(j * 8 + f, 8, stride=0), :]
            ehi, elo = halves(jnp.where(mine, jnp.concatenate([e, e], 0), 0.0))
            lhs_ref[slot, j * 16 : j * 16 + 16, :] = jnp.concatenate([hi, lo, hi, ehi, elo], 1)
        out = sc_ref[slot] + jnp.dot(lhs_ref[slot], w, preferred_element_type=F32)
        for j in range(ROWS):
            for h in range(2):
                res_ref[f, pl.ds(row_of(j, h), PLANES, stride=64), :] = out[j * 16 : j * 16 + 16, 128 * h : 128 * h + 128]
        copy = pltpu.make_async_copy(res_ref.at[f], o_ref.at[f], sem.at[f])
        copy.start()
        copies.append(copy)
    for copy in copies:
        copy.wait()


def params():
    return pltpu.CompilerParams(vmem_limit_bytes=24 * 1024 * 1024)


VM = pl.BlockSpec(memory_space=pltpu.VMEM)


def local(cotangent, lower, pivot, speed):
    stencil, edge = tables()
    sds = jax.ShapeDtypeStruct
    flat = cotangent.reshape(FIELDS, PLANES, 4, 8, 2, 128).transpose(0, 1, 2, 4, 3, 5).reshape(FIELDS, 1024, 128)
    left, right = pl.pallas_call(
        edge_kernel,
        out_shape=[sds((FIELDS, 8, 128), F32)] * 2,
        in_specs=[VM] * 2,
        out_specs=[VM] * 2,
        compiler_params=params(),
        name="edge",
    )(flat, jnp.asarray(edge))
    count = lax.axis_size("stream")
    from_left = lax.ppermute(right, "stream", [(i, (i + 1) % count) for i in range(count)])
    from_right = lax.ppermute(left, "stream", [((i + 1) % count, i) for i in range(count)])
    main, rise, fall, unit = pl.pallas_call(
        sums_kernel,
        out_shape=[sds((WALLS * 16, 128), F32), sds((ROWS * 8, 128), F32), sds((ROWS * 8, 128), F32), sds((2, 8, 128), F32)],
        in_specs=[VM] * 3,
        out_specs=[VM] * 4,
        compiler_params=params(),
        cost_estimate=pl.CostEstimate(flops=4000000, bytes_accessed=2600000, transcendentals=0),
        name="sums",
    )(flat, lower, pivot)
    send, ext = pl.pallas_call(
        merge_kernel,
        out_shape=[sds((WALLS, 16, 128), F32), sds((8, ROWS, 128), F32)],
        in_specs=[VM] * 6,
        out_specs=[VM] * 2,
        compiler_params=params(),
        name="merge",
    )(main, rise, fall, unit, from_left, from_right)
    got = lax.all_to_all(send, "wall", 0, 0, tiled=True)
    carries = pl.pallas_call(
        carry_kernel,
        out_shape=sds((WALLS, 16, 128), F32),
        in_specs=[VM],
        out_specs=VM,
        scratch_shapes=[pltpu.VMEM((WALLS, 8, 128), F32)] * 2,
        compiler_params=params(),
        name="carry",
    )(got)
    back = lax.all_to_all(carries, "wall", 0, 0, tiled=True)
    out = pl.pallas_call(
        final_kernel,
        out_shape=sds((FIELDS, 1024, 128), F32),
        in_specs=[VM] * 7,
        out_specs=pl.BlockSpec(memory_space=pl.ANY),
        scratch_shapes=[pltpu.VMEM((ROWS * 8, 128), F32)] * 4
        + [
            pltpu.VMEM((2, ROWS * PLANES, CELLS), F32),
            pltpu.VMEM((2, ROWS * PLANES, 1024), BF16),
            pltpu.VMEM((FIELDS, 1024, 128), F32),
            pltpu.SemaphoreType.DMA((FIELDS,)),
        ],
        compiler_params=params(),
        name="final",
    )(flat, back.reshape(WALLS * 16, 128), lower, pivot, speed, ext.reshape(8 * ROWS, 128), jnp.asarray(stencil))
    return out.reshape(FIELDS, PLANES, 4, 2, 8, 128).transpose(0, 1, 2, 4, 3, 5).reshape(FIELDS, PLANES, ROWS, CELLS)


def solution(mesh):
    return jax.shard_map(
        local,
        mesh=mesh,
        in_specs=(P(None, None, "wall", "stream"), P(None, "wall"), P(None, "wall"), P(None, "wall")),
        out_specs=P(None, None, "wall", "stream"),
        check_vma=False,
    )
```

```python
import math

import jax
import jax.numpy as jnp
import ml_dtypes
import numpy as np
from jax import lax
from jax.experimental import pallas as pl
from jax.experimental.pallas import tpu as pltpu
from jax.sharding import PartitionSpec as P

F32, BF16 = jnp.float32, jnp.bfloat16
R = (math.sqrt(5.0) - 3.0) / 2.0
GAIN = 3.0 / math.sqrt(5.0)
C1 = 7.0 / 9.0
C2 = 1.0 / 36.0
FIELDS, PLANES, ROWS, CELLS, WALLS = 5, 16, 32, 256, 32


def split_np(w):
    w = np.asarray(w, np.float64)
    hi = w.astype(ml_dtypes.bfloat16)
    lo = (w - hi.astype(np.float64)).astype(ml_dtypes.bfloat16)
    return hi, lo


def tables():
    dec = lambda n: np.where(np.abs(n) % 2 == 0, 1.0, -1.0) * np.abs(R) ** np.abs(n)
    off = np.arange(CELLS)[:, None] - np.arange(CELLS)[None, :]
    tap = lambda o: GAIN * (C1 * (dec(o - 1) - dec(o + 1)) + C2 * (dec(o - 2) - dec(o + 2)))
    whi, wlo = split_np(tap(off))
    kappa = GAIN * (C1 * (1.0 / R - R) + C2 * (R**-2 - R**2))
    corr = tap(np.array(-1)) + kappa * R
    x = np.arange(CELLS)
    ext = np.zeros((4, CELLS))
    ext[0] = kappa * dec(CELLS - x)
    ext[1, CELLS - 1] = -corr
    ext[2] = -kappa * dec(x + 1)
    ext[3, 0] = corr
    ehi, elo = split_np(np.repeat(ext, PLANES, axis=0))
    zero = np.zeros_like(elo)
    stencil = np.concatenate([whi, whi, wlo, ehi, elo, ehi, zero], axis=0)
    edge = np.zeros((CELLS, 4))
    edge[:, 0] = dec(x)
    edge[0, 1] = 1.0
    edge[:, 2] = dec(CELLS - 1 - x)
    edge[CELLS - 1, 3] = 1.0
    edge = np.concatenate([np.repeat(edge, PLANES, axis=1), np.zeros((CELLS, 64))], axis=1)
    ghi, glo = split_np(edge)
    return stencil, np.concatenate([ghi, ghi, glo], axis=0)


def halves(x):
    hi = x.astype(BF16)
    return hi, (x - hi.astype(F32)).astype(BF16)


def lanes(shape):
    return lax.broadcasted_iota(jnp.int32, shape, len(shape) - 1)


def sublanes(shape):
    return lax.broadcasted_iota(jnp.int32, shape, len(shape) - 2)


def edge_kernel(c_hbm, w_hbm, lower_hbm, pivot_hbm, left_ref, right_ref, c_ref, rise_ref, fall_ref, unit_ref, w_ref, lower_ref, pivot_ref, sem):
    small = [
        pltpu.make_async_copy(a, b, sem.at[FIELDS + i])
        for i, (a, b) in enumerate([(lower_hbm, lower_ref), (pivot_hbm, pivot_ref), (w_hbm, w_ref)])
    ]
    big = [pltpu.make_async_copy(c_hbm.at[f], c_ref.at[f], sem.at[f]) for f in range(FIELDS)]
    for copy in small + big:
        copy.start()
    small[0].wait()
    small[1].wait()
    weights(lower_ref, pivot_ref, rise_ref, fall_ref, unit_ref)
    small[2].wait()
    w = w_ref[...]
    lane32, lane = lanes((ROWS, 128)) % 16, lanes((8, 128)) // 32
    for f in range(FIELDS):
        big[f].wait()
        tiles = c_ref[f].reshape(PLANES * 4, 2, 8, 128)
        rows = [tiles[:, h].reshape(PLANES * ROWS, 128) for h in range(2)]
        hi, lo = halves(jnp.concatenate(rows, axis=1))
        sums = jnp.dot(jnp.concatenate([hi, lo, hi], axis=1), w, preferred_element_type=F32)
        own = sums[:ROWS]
        for p in range(1, PLANES):
            own = jnp.where(lane32 == p, sums[p * ROWS : (p + 1) * ROWS], own)
        left = own[:8]
        right = pltpu.roll(own[:8], 96, 1)
        for q in range(1, 4):
            part = own[8 * q : 8 * q + 8]
            left = jnp.where(lane == q, pltpu.roll(part, 32 * q, 1), left)
            right = jnp.where(lane == q, pltpu.roll(part, (32 * q + 96) % 128, 1) if q != 1 else part, right)
        left_ref[f] = left
        right_ref[f] = right


def row_of(j, h):
    return (j // 8) * 16 + h * 8 + j % 8


def load_row(ref, f, j):
    return jnp.concatenate([ref[f, pl.ds(row_of(j, h), PLANES, stride=64), :] for h in range(2)], 1)


def full(ref, j, f):
    v = ref[pl.ds(j * 8 + f, 8, stride=0), :]
    return jnp.concatenate([jnp.concatenate([v, v], 0)] * 2, 1)


def spread_rows(ref, out_ref):
    value = ref[...]
    for j in range(ROWS):
        out_ref[j * 8 : j * 8 + FIELDS, :] = jnp.broadcast_to(value[:, j : j + 1], (FIELDS, 128))


def weights(lower_ref, pivot_ref, rise_ref, fall_ref, unit_ref):
    low, piv = lower_ref[...], 1.0 / pivot_ref[...]
    wide = lambda v, j: jnp.broadcast_to(v[:, j : j + 1], (FIELDS, 128))
    entry = jnp.ones((FIELDS, 128), F32)
    direct, spread = [], jnp.zeros((FIELDS, 128), F32)
    for j in range(ROWS):
        direct.append(entry * wide(piv, j))
        spread = spread + entry * direct[j]
        entry = entry * wide(low, j)
    leave, first = None, None
    for j in reversed(range(ROWS)):
        l = wide(low, j)
        leave = l if leave is None else l * leave
        first = direct[j] if first is None else direct[j] + l * first
        rise_ref[j * 8 : j * 8 + FIELDS, :] = leave
        fall_ref[j * 8 : j * 8 + FIELDS, :] = first
    unit_ref[0, :FIELDS, :] = entry
    unit_ref[1, :FIELDS, :] = spread


def sums_kernel(c_ref, rise_ref, fall_ref, out_ref):
    for f in range(FIELDS):
        up = jnp.zeros((PLANES, CELLS), F32)
        down = jnp.zeros((PLANES, CELLS), F32)
        for j in range(ROWS):
            v = load_row(c_ref, f, j)
            up = up + full(rise_ref, j, f) * v
            down = down + full(fall_ref, j, f) * v
        for h in range(2):
            for q in range(2):
                base = (16 * q + h) * 16 + f
                out_ref[pl.ds(base, 8, stride=32), :] = up[8 * q : 8 * q + 8, 128 * h : 128 * h + 128]
                out_ref[pl.ds(base + 8, 8, stride=32), :] = down[8 * q : 8 * q + 8, 128 * h : 128 * h + 128]


def merge_kernel(main_ref, rise_ref, fall_ref, unit_ref, left_ref, right_ref, out_ref, ext_ref):
    lane = lanes((8, 128))
    ups, downs = [], []
    for f in range(FIELDS):
        up = jnp.zeros((8, 128), F32)
        down = jnp.zeros((8, 128), F32)
        from_left, from_right = left_ref[f], right_ref[f]
        for q in range(4):
            r = pltpu.roll(from_right, (128 - 32 * q) % 128, 1) if q else from_right
            l = pltpu.roll(from_left, (128 - 32 * q + 32) % 128, 1) if q != 1 else from_left
            v = jnp.where(lane < 32, r, l)
            v = jnp.where(lane < 64, v, pltpu.roll(v, 64, 1))
            ext_ref[f, 8 * q : 8 * q + 8, :] = v
            up = up + rise_ref[pl.ds(64 * q + f, 8, stride=8), :] * v
            down = down + fall_ref[pl.ds(64 * q + f, 8, stride=8), :] * v
        ups.append(jnp.sum(up, axis=0, keepdims=True))
        downs.append(jnp.sum(down, axis=0, keepdims=True))
    for f in range(FIELDS, 8):
        ext_ref[f] = jnp.zeros((ROWS, 128), F32)
    row = sublanes((FIELDS, 128))
    lane5 = lanes((FIELDS, 128))
    coef = jnp.where(lane5 == 64 + row, unit_ref[0, :FIELDS, :], 0.0)
    coef = jnp.where(lane5 == 72 + row, unit_ref[1, :FIELDS, :], coef)
    coef = jnp.sum(coef, axis=0, keepdims=True)
    lane1 = lanes((1, 128))
    sub = sublanes((8, 128))

    def pack(v, last):
        rows = [jnp.where(lane1 < 64, v[0], v[1]), jnp.where(lane1 < 64, v[2], v[3]), jnp.where(lane1 < 64, v[4], last)]
        return jnp.where(sub == 5, rows[0], jnp.where(sub == 6, rows[1], rows[2]))

    tail_up, tail_down = pack(ups, coef), pack(downs, jnp.zeros((1, 128), F32))
    for k in range(WALLS):
        out_ref[k, :8, :] = jnp.where(sub < 5, main_ref[16 * k : 16 * k + 8, :], tail_up)
        out_ref[k, 8:, :] = jnp.where(sub < 5, main_ref[16 * k + 8 : 16 * k + 16, :], tail_down)


def carry_kernel(in_ref, out_ref, through_ref, crest_ref):
    sub, lane = sublanes((8, 128)), lanes((8, 128))
    low_field = jnp.where(sub < 5, sub, 2 * (sub - 5))
    high_field = jnp.where(sub < 5, sub, jnp.where(sub < 7, 2 * (sub - 5) + 1, 4))

    def pick(row, at):
        lo = jnp.sum(jnp.where(lane == at + low_field, row, 0.0), axis=1, keepdims=True)
        hi = jnp.sum(jnp.where(lane == at + high_field, row, 0.0), axis=1, keepdims=True)
        return jnp.where(lane < 64, lo, hi)

    run = jnp.zeros((8, 128), F32)
    for d in range(WALLS):
        row = jnp.broadcast_to(in_ref[d, 7:8, :], (8, 128))
        through, spread = pick(row, 64), pick(row, 72)
        through_ref[d] = through
        out_ref[d, :8, :] = run
        crest_ref[d] = in_ref[d, 8:, :] + spread * run
        run = through * run + in_ref[d, :8, :]
    run = jnp.zeros((8, 128), F32)
    for d in reversed(range(WALLS)):
        out_ref[d, 8:, :] = run
        run = through_ref[d] * run + crest_ref[d]


def final_kernel(c_ref, ret_ref, lower_ref, pivot_ref, speed_ref, ext_ref, w_ref, o_ref, low_ref, inv_ref, sp_ref, fe_ref, fl_ref, sc_ref, lhs_ref, res_ref, sem):
    spread_rows(lower_ref, low_ref)
    spread_rows(speed_ref, sp_ref)
    value = 1.0 / pivot_ref[...]
    for j in range(ROWS):
        inv_ref[j * 8 : j * 8 + FIELDS, :] = jnp.broadcast_to(value[:, j : j + 1], (FIELDS, 128))
    sub, lane = sublanes((8, 128)), lanes((8, 128))

    def unpack(tile):
        turned = pltpu.roll(tile, 64, 1)
        a, b = jnp.where(lane < 64, tile, turned), jnp.where(lane < 64, turned, tile)
        rows = [a[5:6], b[5:6], a[6:7], b[6:7], a[7:8]]
        out = jnp.broadcast_to(rows[4], (8, 128))
        for f in range(4):
            out = jnp.where(sub == f, rows[f], out)
        return jnp.where(sub < FIELDS, out, 0.0)

    run = unpack(ret_ref[0:8, :])
    for j in range(ROWS):
        run = ext_ref[pl.ds(j, 8, stride=ROWS), :] + run
        fe_ref[j * 8 : j * 8 + 8, :] = run * inv_ref[j * 8 : j * 8 + 8, :]
        run = run * low_ref[j * 8 : j * 8 + 8, :]
    run = unpack(ret_ref[8:16, :])
    for j in reversed(range(ROWS)):
        run = fe_ref[j * 8 : j * 8 + 8, :] + low_ref[j * 8 : j * 8 + 8, :] * run
        fe_ref[j * 8 : j * 8 + 8, :] = run * sp_ref[j * 8 : j * 8 + 8, :]

    for j in range(ROWS):
        hi, lo = halves(fe_ref[j * 8 : j * 8 + 8, :])
        fe_ref[j * 8 : j * 8 + 8, :] = hi.astype(F32)
        fl_ref[j * 8 : j * 8 + 8, :] = lo.astype(F32)

    mine = lanes((PLANES, 128)) % 16 == sublanes((PLANES, 128))
    w = w_ref[...]

    def carry(f, shift):
        parts = [[ret_ref[pl.ds((16 * q + h) * 16 + f + shift, 8, stride=32), :] for h in range(2)] for q in range(2)]
        return jnp.concatenate([jnp.concatenate(p, 1) for p in parts], 0)

    def planes(ref, j, f):
        v = ref[pl.ds(j * 8 + f, 8, stride=0), :]
        return jnp.where(mine, jnp.concatenate([v, v], 0), 0.0).astype(BF16)

    run = [carry(f, 0) for f in range(FIELDS)]
    for j in range(ROWS):
        for f in range(FIELDS):
            now = load_row(c_ref, f, j) + run[f]
            sc_ref[f, j * 16 : j * 16 + 16, :] = now * full(inv_ref, j, f)
            run[f] = now * full(low_ref, j, f)
    run = [carry(f, 8) for f in range(FIELDS)]
    copies = []
    for t in reversed(range(4)):
        for j in reversed(range(8 * t, 8 * t + 8)):
            for f in range(FIELDS):
                run[f] = sc_ref[f, j * 16 : j * 16 + 16, :] + full(low_ref, j, f) * run[f]
                sc_ref[f, j * 16 : j * 16 + 16, :] = run[f]
                hi, lo = halves(run[f] * full(sp_ref, j, f))
                at = f * 128 + (j % 8) * 16
                lhs_ref[t % 2, at : at + 16, :] = jnp.concatenate([hi, lo, hi, planes(fe_ref, j, f), planes(fl_ref, j, f)], 1)
        out = jnp.dot(lhs_ref[t % 2], w, preferred_element_type=F32)
        for f in range(FIELDS):
            for s in range(8):
                j, at = 8 * t + s, f * 128 + s * 16
                value = out[at : at + 16] + sc_ref[f, j * 16 : j * 16 + 16, :]
                for h in range(2):
                    res_ref[t, pl.ds(f * 256 + h * 8 + s, PLANES, stride=16), :] = value[:, 128 * h : 128 * h + 128]
        copy = pltpu.make_async_copy(res_ref.at[t].reshape(FIELDS * PLANES, 16, 128), o_ref.at[:, t], sem.at[t])
        copy.start()
        copies.append(copy)
    for copy in copies:
        copy.wait()


def params():
    return pltpu.CompilerParams(vmem_limit_bytes=24 * 1024 * 1024)


VM = pl.BlockSpec(memory_space=pltpu.VMEM)


def local(cotangent, lower, pivot, speed):
    stencil, edge = tables()
    sds = jax.ShapeDtypeStruct
    flat = cotangent.reshape(FIELDS, PLANES, 4, 8, 2, 128).transpose(0, 1, 2, 4, 3, 5).reshape(FIELDS, 1024, 128)
    rows = sds((ROWS * 8, 128), F32)
    left, right, cells, rise, fall, unit = pl.pallas_call(
        edge_kernel,
        out_shape=[sds((FIELDS, 8, 128), F32)] * 2 + [sds((FIELDS, 1024, 128), F32), rows, rows, sds((2, 8, 128), F32)],
        in_specs=[pl.BlockSpec(memory_space=pl.ANY)] * 4,
        out_specs=[VM] * 6,
        scratch_shapes=[
            pltpu.VMEM((3 * CELLS, 128), BF16),
            pltpu.VMEM((FIELDS, ROWS), F32),
            pltpu.VMEM((FIELDS, ROWS), F32),
            pltpu.SemaphoreType.DMA((FIELDS + 3,)),
        ],
        compiler_params=params(),
        name="edge",
    )(flat, jnp.asarray(edge), lower, pivot)
    count = lax.axis_size("stream")
    from_left = lax.ppermute(right, "stream", [(i, (i + 1) % count) for i in range(count)])
    from_right = lax.ppermute(left, "stream", [((i + 1) % count, i) for i in range(count)])
    main = pl.pallas_call(
        sums_kernel,
        out_shape=sds((WALLS * 16, 128), F32),
        in_specs=[VM] * 3,
        out_specs=VM,
        compiler_params=params(),
        cost_estimate=pl.CostEstimate(flops=4000000, bytes_accessed=2600000, transcendentals=0),
        name="sums",
    )(cells, rise, fall)
    send, ext = pl.pallas_call(
        merge_kernel,
        out_shape=[sds((WALLS, 16, 128), F32), sds((8, ROWS, 128), F32)],
        in_specs=[VM] * 6,
        out_specs=[VM] * 2,
        compiler_params=params(),
        name="merge",
    )(main, rise, fall, unit, from_left, from_right)
    got = lax.all_to_all(send, "wall", 0, 0, tiled=True)
    carries = pl.pallas_call(
        carry_kernel,
        out_shape=sds((WALLS, 16, 128), F32),
        in_specs=[VM],
        out_specs=VM,
        scratch_shapes=[pltpu.VMEM((WALLS, 8, 128), F32)] * 2,
        compiler_params=params(),
        name="carry",
    )(got)
    back = lax.all_to_all(carries, "wall", 0, 0, tiled=True)
    out = pl.pallas_call(
        final_kernel,
        out_shape=sds((FIELDS * PLANES, 4, 16, 128), F32),
        in_specs=[VM] * 7,
        out_specs=pl.BlockSpec(memory_space=pl.ANY),
        scratch_shapes=[pltpu.VMEM((ROWS * 8, 128), F32)] * 5
        + [
            pltpu.VMEM((FIELDS, ROWS * PLANES, CELLS), F32),
            pltpu.VMEM((2, FIELDS * PLANES * 8, 1024), BF16),
            pltpu.VMEM((4, FIELDS * PLANES * 16, 128), F32),
            pltpu.SemaphoreType.DMA((4,)),
        ],
        compiler_params=params(),
        name="final",
    )(cells, back.reshape(WALLS * 16, 128), lower, pivot, speed, ext.reshape(8 * ROWS, 128), jnp.asarray(stencil))
    return out.reshape(FIELDS, PLANES, 4, 2, 8, 128).transpose(0, 1, 2, 4, 3, 5).reshape(FIELDS, PLANES, ROWS, CELLS)


def solution(mesh):
    return jax.shard_map(
        local,
        mesh=mesh,
        in_specs=(P(None, None, "wall", "stream"), P(None, "wall"), P(None, "wall"), P(None, "wall")),
        out_specs=P(None, None, "wall", "stream"),
        check_vma=False,
    )
```

```python
import math

import jax
import jax.numpy as jnp
import ml_dtypes
import numpy as np
from jax import lax
from jax.experimental import pallas as pl
from jax.experimental.pallas import tpu as pltpu
from jax.sharding import PartitionSpec as P

F32, BF16 = jnp.float32, jnp.bfloat16
R = (math.sqrt(5.0) - 3.0) / 2.0
GAIN = 3.0 / math.sqrt(5.0)
C1 = 7.0 / 9.0
C2 = 1.0 / 36.0
FIELDS, PLANES, ROWS, CELLS, WALLS = 5, 16, 32, 256, 32


def split_np(w):
    w = np.asarray(w, np.float64)
    hi = w.astype(ml_dtypes.bfloat16)
    lo = (w - hi.astype(np.float64)).astype(ml_dtypes.bfloat16)
    return hi, lo


def tables():
    dec = lambda n: np.where(np.abs(n) % 2 == 0, 1.0, -1.0) * np.abs(R) ** np.abs(n)
    off = np.arange(CELLS)[:, None] - np.arange(CELLS)[None, :]
    tap = lambda o: GAIN * (C1 * (dec(o - 1) - dec(o + 1)) + C2 * (dec(o - 2) - dec(o + 2)))
    whi, wlo = split_np(tap(off))
    kappa = GAIN * (C1 * (1.0 / R - R) + C2 * (R**-2 - R**2))
    corr = tap(np.array(-1)) + kappa * R
    x = np.arange(CELLS)
    ext = np.zeros((4, CELLS))
    ext[0] = kappa * dec(CELLS - x)
    ext[1, CELLS - 1] = -corr
    ext[2] = -kappa * dec(x + 1)
    ext[3, 0] = corr
    ehi, elo = split_np(np.repeat(ext, PLANES, axis=0))
    zero = np.zeros_like(elo)
    stencil = np.concatenate([whi, whi, wlo, ehi, elo, ehi, zero], axis=0)
    edge = np.zeros((CELLS, 4))
    edge[:, 0] = dec(x)
    edge[0, 1] = 1.0
    edge[:, 2] = dec(CELLS - 1 - x)
    edge[CELLS - 1, 3] = 1.0
    edge = np.concatenate([np.repeat(edge, PLANES, axis=1), np.zeros((CELLS, 64))], axis=1)
    ghi, glo = split_np(edge)
    return stencil, np.concatenate([ghi, ghi, glo], axis=0)


def halves(x):
    hi = x.astype(BF16)
    return hi, (x - hi.astype(F32)).astype(BF16)


def lanes(shape):
    return lax.broadcasted_iota(jnp.int32, shape, len(shape) - 1)


def sublanes(shape):
    return lax.broadcasted_iota(jnp.int32, shape, len(shape) - 2)


def edge_kernel(c_hbm, w_hbm, lower_hbm, pivot_hbm, left_ref, right_ref, c_ref, rise_ref, fall_ref, unit_ref, w_ref, lower_ref, pivot_ref, sem):
    small = [
        pltpu.make_async_copy(a, b, sem.at[i])
        for i, (a, b) in enumerate([(lower_hbm, lower_ref), (pivot_hbm, pivot_ref), (w_hbm, w_ref)])
    ]
    big = [
        [
            pltpu.make_async_copy(c_hbm.at[f, :, t, h], c_ref.at[f, t, h], sem.at[3 + (f * 4 + t) * 2 + h])
            for t in range(4)
            for h in range(2)
        ]
        for f in range(FIELDS)
    ]
    for copy in small + sum(big, []):
        copy.start()
    small[0].wait()
    small[1].wait()
    weights(lower_ref, pivot_ref, rise_ref, fall_ref, unit_ref)
    small[2].wait()
    w = w_ref[...]
    plane, lane = lanes((8, 128)) % 16, lanes((8, 128)) // 32
    for f in range(FIELDS):
        for copy in big[f]:
            copy.wait()
        rows = [c_ref[f, :, h].reshape(PLANES * ROWS, 128) for h in range(2)]
        hi, lo = halves(jnp.concatenate(rows, axis=1))
        sums = jnp.dot(jnp.concatenate([hi, lo, hi], axis=1), w, preferred_element_type=F32)
        own = []
        for t in range(4):
            part = sums[t * 128 : t * 128 + 8]
            for p in range(1, PLANES):
                part = jnp.where(plane == p, sums[t * 128 + p * 8 : t * 128 + p * 8 + 8], part)
            own.append(part)
        left = own[0]
        right = pltpu.roll(own[0], 96, 1)
        for q in range(1, 4):
            part = own[q]
            left = jnp.where(lane == q, pltpu.roll(part, 32 * q, 1), left)
            right = jnp.where(lane == q, pltpu.roll(part, (32 * q + 96) % 128, 1) if q != 1 else part, right)
        left_ref[f] = left
        right_ref[f] = right


def load_row(ref, f, t, s):
    return jnp.concatenate([ref[f, pl.ds(t * 256 + h * 128 + s, PLANES, stride=8), :] for h in range(2)], 1)


def full(ref, j, f):
    v = ref[pl.ds(j * 8 + f, 8, stride=0), :]
    return jnp.concatenate([jnp.concatenate([v, v], 0)] * 2, 1)


def spread_rows(ref, out_ref):
    value = ref[...]
    for j in range(ROWS):
        out_ref[j * 8 : j * 8 + FIELDS, :] = jnp.broadcast_to(value[:, j : j + 1], (FIELDS, 128))


def weights(lower_ref, pivot_ref, rise_ref, fall_ref, unit_ref):
    low, piv = lower_ref[...], 1.0 / pivot_ref[...]
    wide = lambda v, j: jnp.broadcast_to(v[:, j : j + 1], (FIELDS, 128))
    entry = jnp.ones((FIELDS, 128), F32)
    direct, spread = [], jnp.zeros((FIELDS, 128), F32)
    for j in range(ROWS):
        direct.append(entry * wide(piv, j))
        spread = spread + entry * direct[j]
        entry = entry * wide(low, j)
    leave, first = None, None
    for j in reversed(range(ROWS)):
        l = wide(low, j)
        leave = l if leave is None else l * leave
        first = direct[j] if first is None else direct[j] + l * first
        rise_ref[j * 8 : j * 8 + FIELDS, :] = leave
        fall_ref[j * 8 : j * 8 + FIELDS, :] = first
    unit_ref[0, :FIELDS, :] = entry
    unit_ref[1, :FIELDS, :] = spread


def sums_kernel(c_ref, rise_ref, fall_ref, out_ref):
    for f in range(FIELDS):
        up = jnp.zeros((PLANES, CELLS), F32)
        down = jnp.zeros((PLANES, CELLS), F32)
        for j in range(ROWS):
            v = load_row(c_ref, f, j // 8, j % 8)
            up = up + full(rise_ref, j, f) * v
            down = down + full(fall_ref, j, f) * v
        for h in range(2):
            for q in range(2):
                base = (16 * h + 8 * q) * 16 + f
                out_ref[pl.ds(base, 8, stride=16), :] = up[8 * q : 8 * q + 8, 128 * h : 128 * h + 128]
                out_ref[pl.ds(base + 8, 8, stride=16), :] = down[8 * q : 8 * q + 8, 128 * h : 128 * h + 128]


def merge_kernel(main_ref, rise_ref, fall_ref, unit_ref, left_ref, right_ref, out_ref, ext_ref):
    lane = lanes((8, 128))
    ups, downs = [], []
    for f in range(FIELDS):
        up = jnp.zeros((8, 128), F32)
        down = jnp.zeros((8, 128), F32)
        from_left, from_right = left_ref[f], right_ref[f]
        for q in range(4):
            r = pltpu.roll(from_right, (128 - 32 * q) % 128, 1) if q else from_right
            l = pltpu.roll(from_left, (128 - 32 * q + 32) % 128, 1) if q != 1 else from_left
            v = jnp.where(lane < 32, r, l)
            v = jnp.where(lane < 64, v, pltpu.roll(v, 64, 1))
            ext_ref[pl.ds(64 * q + f, 8, stride=8), :] = v
            up = up + rise_ref[pl.ds(64 * q + f, 8, stride=8), :] * v
            down = down + fall_ref[pl.ds(64 * q + f, 8, stride=8), :] * v
        ups.append(jnp.sum(up, axis=0, keepdims=True))
        downs.append(jnp.sum(down, axis=0, keepdims=True))
    row = sublanes((FIELDS, 128))
    lane5 = lanes((FIELDS, 128))
    coef = jnp.where(lane5 == 64 + row, unit_ref[0, :FIELDS, :], 0.0)
    coef = jnp.where(lane5 == 72 + row, unit_ref[1, :FIELDS, :], coef)
    coef = jnp.sum(coef, axis=0, keepdims=True)
    lane1 = lanes((1, 128))
    sub = sublanes((8, 128))

    def pack(v, last):
        rows = [jnp.where(lane1 < 64, v[0], v[1]), jnp.where(lane1 < 64, v[2], v[3]), jnp.where(lane1 < 64, v[4], last)]
        return jnp.where(sub == 5, rows[0], jnp.where(sub == 6, rows[1], rows[2]))

    tail_up, tail_down = pack(ups, coef), pack(downs, jnp.zeros((1, 128), F32))
    for k in range(WALLS):
        out_ref[k, :8, :] = jnp.where(sub < 5, main_ref[16 * k : 16 * k + 8, :], tail_up)
        out_ref[k, 8:, :] = jnp.where(sub < 5, main_ref[16 * k + 8 : 16 * k + 16, :], tail_down)


def carry_kernel(in_ref, out_ref, through_ref, crest_ref):
    sub, lane = sublanes((8, 128)), lanes((8, 128))
    low_field = jnp.where(sub < 5, sub, 2 * (sub - 5))
    high_field = jnp.where(sub < 5, sub, jnp.where(sub < 7, 2 * (sub - 5) + 1, 4))

    def pick(row, at):
        lo = jnp.sum(jnp.where(lane == at + low_field, row, 0.0), axis=1, keepdims=True)
        hi = jnp.sum(jnp.where(lane == at + high_field, row, 0.0), axis=1, keepdims=True)
        return jnp.where(lane < 64, lo, hi)

    run = jnp.zeros((8, 128), F32)
    for d in range(WALLS):
        row = jnp.broadcast_to(in_ref[d, 7:8, :], (8, 128))
        through, spread = pick(row, 64), pick(row, 72)
        through_ref[d] = through
        out_ref[d, :8, :] = run
        crest_ref[d] = in_ref[d, 8:, :] + spread * run
        run = through * run + in_ref[d, :8, :]
    run = jnp.zeros((8, 128), F32)
    for d in reversed(range(WALLS)):
        out_ref[d, 8:, :] = run
        run = through_ref[d] * run + crest_ref[d]


def final_kernel(c_ref, ret_ref, lower_ref, pivot_ref, speed_ref, ext_ref, w_ref, o_ref, low_ref, inv_ref, sp_ref, fe_ref, fl_ref, sc_ref, lhs_ref, res_ref, sem):
    spread_rows(lower_ref, low_ref)
    spread_rows(speed_ref, sp_ref)
    value = 1.0 / pivot_ref[...]
    for j in range(ROWS):
        inv_ref[j * 8 : j * 8 + FIELDS, :] = jnp.broadcast_to(value[:, j : j + 1], (FIELDS, 128))
    sub, lane = sublanes((8, 128)), lanes((8, 128))

    def unpack(tile):
        turned = pltpu.roll(tile, 64, 1)
        a, b = jnp.where(lane < 64, tile, turned), jnp.where(lane < 64, turned, tile)
        rows = [a[5:6], b[5:6], a[6:7], b[6:7], a[7:8]]
        out = jnp.broadcast_to(rows[4], (8, 128))
        for f in range(4):
            out = jnp.where(sub == f, rows[f], out)
        return jnp.where(sub < FIELDS, out, 0.0)

    run = unpack(ret_ref[0:8, :])
    for j in range(ROWS):
        run = ext_ref[j * 8 : j * 8 + 8, :] + run
        fe_ref[j * 8 : j * 8 + 8, :] = run * inv_ref[j * 8 : j * 8 + 8, :]
        run = run * low_ref[j * 8 : j * 8 + 8, :]
    run = unpack(ret_ref[8:16, :])
    for j in reversed(range(ROWS)):
        run = fe_ref[j * 8 : j * 8 + 8, :] + low_ref[j * 8 : j * 8 + 8, :] * run
        fe_ref[j * 8 : j * 8 + 8, :] = run * sp_ref[j * 8 : j * 8 + 8, :]

    for j in range(ROWS):
        hi, lo = halves(fe_ref[j * 8 : j * 8 + 8, :])
        fe_ref[j * 8 : j * 8 + 8, :] = hi.astype(F32)
        fl_ref[j * 8 : j * 8 + 8, :] = lo.astype(F32)

    mine = lanes((PLANES, 128)) % 16 == sublanes((PLANES, 128))
    w = w_ref[...]

    def carry(f, shift):
        parts = [[ret_ref[pl.ds((16 * h + 8 * q) * 16 + f + shift, 8, stride=16), :] for h in range(2)] for q in range(2)]
        return jnp.concatenate([jnp.concatenate(p, 1) for p in parts], 0)

    def planes(ref, j, f):
        v = ref[pl.ds(j * 8 + f, 8, stride=0), :]
        return jnp.where(mine, jnp.concatenate([v, v], 0), 0.0).astype(BF16)

    def rise(t, run):
        run = list(run)
        for s in range(8):
            for f in range(FIELDS):
                now = load_row(c_ref, f, t, s) + run[f]
                sc_ref[f, pl.ds(pl.multiple_of(t * 128, 128) + s * 16, 16), :] = now * full(inv_ref, t * 8 + s, f)
                run[f] = now * full(low_ref, t * 8 + s, f)
        return tuple(run)

    lax.fori_loop(0, 4, rise, tuple(carry(f, 0) for f in range(FIELDS)))
    run = [carry(f, 8) for f in range(FIELDS)]
    copies = []
    for t in reversed(range(4)):
        for j in reversed(range(8 * t, 8 * t + 8)):
            for f in range(FIELDS):
                run[f] = sc_ref[f, j * 16 : j * 16 + 16, :] + full(low_ref, j, f) * run[f]
                sc_ref[f, j * 16 : j * 16 + 16, :] = run[f]
                hi, lo = halves(run[f] * full(sp_ref, j, f))
                at = f * 128 + (j % 8) * 16
                lhs_ref[t % 2, at : at + 16, :] = jnp.concatenate([hi, lo, hi, planes(fe_ref, j, f), planes(fl_ref, j, f)], 1)
        out = jnp.dot(lhs_ref[t % 2], w, preferred_element_type=F32)
        for f in range(FIELDS):
            for s in range(8):
                j, at = 8 * t + s, f * 128 + s * 16
                value = out[at : at + 16] + sc_ref[f, j * 16 : j * 16 + 16, :]
                for h in range(2):
                    res_ref[t, h, pl.ds(f * 128 + s, PLANES, stride=8), :] = value[:, 128 * h : 128 * h + 128]
        for h in range(2):
            source = res_ref.at[t, h].reshape(FIELDS * PLANES, 8, 128)
            copies.append(pltpu.make_async_copy(source, o_ref.at[:, t, h], sem.at[2 * t + h]))
            copies[-1].start()
    for copy in copies:
        copy.wait()


def params():
    return pltpu.CompilerParams(vmem_limit_bytes=24 * 1024 * 1024)


VM = pl.BlockSpec(memory_space=pltpu.VMEM)


def local(cotangent, lower, pivot, speed):
    stencil, edge = tables()
    sds = jax.ShapeDtypeStruct
    flat = cotangent.reshape(FIELDS, PLANES, 4, 8, 2, 128).transpose(0, 1, 2, 4, 3, 5)
    rows = sds((ROWS * 8, 128), F32)
    left, right, cells, rise, fall, unit = pl.pallas_call(
        edge_kernel,
        out_shape=[sds((FIELDS, 8, 128), F32)] * 2 + [sds((FIELDS, 4, 2, PLANES, 8, 128), F32), rows, rows, sds((2, 8, 128), F32)],
        in_specs=[pl.BlockSpec(memory_space=pltpu.HBM)] * 4,
        out_specs=[VM] * 6,
        scratch_shapes=[
            pltpu.VMEM((3 * CELLS, 128), BF16),
            pltpu.VMEM((FIELDS, ROWS), F32),
            pltpu.VMEM((FIELDS, ROWS), F32),
            pltpu.SemaphoreType.DMA((8 * FIELDS + 3,)),
        ],
        compiler_params=params(),
        name="edge",
    )(*[pltpu.with_memory_space_constraint(v, pltpu.HBM) for v in (flat, jnp.asarray(edge), lower, pivot)])
    cells = cells.reshape(FIELDS, 1024, 128)
    count = lax.axis_size("stream")
    from_left = lax.ppermute(right, "stream", [(i, (i + 1) % count) for i in range(count)])
    from_right = lax.ppermute(left, "stream", [((i + 1) % count, i) for i in range(count)])
    main = pl.pallas_call(
        sums_kernel,
        out_shape=sds((WALLS * 16, 128), F32),
        in_specs=[VM] * 3,
        out_specs=VM,
        compiler_params=params(),
        cost_estimate=pl.CostEstimate(flops=4000000, bytes_accessed=2600000, transcendentals=0),
        name="sums",
    )(cells, rise, fall)
    send, ext = pl.pallas_call(
        merge_kernel,
        out_shape=[sds((WALLS, 16, 128), F32), rows],
        in_specs=[VM] * 6,
        out_specs=[VM] * 2,
        compiler_params=params(),
        name="merge",
    )(main, rise, fall, unit, from_left, from_right)
    got = lax.all_to_all(send, "wall", 0, 0, tiled=True)
    carries = pl.pallas_call(
        carry_kernel,
        out_shape=sds((WALLS, 16, 128), F32),
        in_specs=[VM],
        out_specs=VM,
        scratch_shapes=[pltpu.VMEM((WALLS, 8, 128), F32)] * 2,
        compiler_params=params(),
        name="carry",
    )(got)
    back = lax.all_to_all(carries, "wall", 0, 0, tiled=True)
    out = pl.pallas_call(
        final_kernel,
        out_shape=sds((FIELDS * PLANES, 4, 2, 8, 128), F32),
        in_specs=[VM] * 7,
        out_specs=pl.BlockSpec(memory_space=pl.ANY),
        scratch_shapes=[pltpu.VMEM((ROWS * 8, 128), F32)] * 5
        + [
            pltpu.VMEM((FIELDS, ROWS * PLANES, CELLS), F32),
            pltpu.VMEM((2, FIELDS * PLANES * 8, 1024), BF16),
            pltpu.VMEM((4, 2, FIELDS * PLANES * 8, 128), F32),
            pltpu.SemaphoreType.DMA((8,)),
        ],
        compiler_params=params(),
        name="final",
    )(cells, back.reshape(WALLS * 16, 128), lower, pivot, speed, ext, jnp.asarray(stencil))
    return out.reshape(FIELDS, PLANES, 4, 2, 8, 128).transpose(0, 1, 2, 4, 3, 5).reshape(FIELDS, PLANES, ROWS, CELLS)


def solution(mesh):
    return jax.shard_map(
        local,
        mesh=mesh,
        in_specs=(P(None, None, "wall", "stream"), P(None, "wall"), P(None, "wall"), P(None, "wall")),
        out_specs=P(None, None, "wall", "stream"),
        check_vma=False,
    )
```

```python
import math

import jax
import jax.numpy as jnp
import ml_dtypes
import numpy as np
from jax import lax
from jax.experimental import pallas as pl
from jax.experimental.pallas import tpu as pltpu
from jax.sharding import PartitionSpec as P

F32, BF16 = jnp.float32, jnp.bfloat16
R = (math.sqrt(5.0) - 3.0) / 2.0
GAIN = 3.0 / math.sqrt(5.0)
C1 = 7.0 / 9.0
C2 = 1.0 / 36.0
FIELDS, PLANES, ROWS, CELLS, WALLS = 5, 16, 32, 256, 32


def split_np(w):
    w = np.asarray(w, np.float64)
    hi = w.astype(ml_dtypes.bfloat16)
    lo = (w - hi.astype(np.float64)).astype(ml_dtypes.bfloat16)
    return hi, lo


def tables():
    dec = lambda n: np.where(np.abs(n) % 2 == 0, 1.0, -1.0) * np.abs(R) ** np.abs(n)
    off = np.arange(CELLS)[:, None] - np.arange(CELLS)[None, :]
    tap = lambda o: GAIN * (C1 * (dec(o - 1) - dec(o + 1)) + C2 * (dec(o - 2) - dec(o + 2)))
    whi, wlo = split_np(tap(off))
    kappa = GAIN * (C1 * (1.0 / R - R) + C2 * (R**-2 - R**2))
    corr = tap(np.array(-1)) + kappa * R
    x = np.arange(CELLS)
    ext = np.zeros((4, CELLS))
    ext[0] = kappa * dec(CELLS - x)
    ext[1, CELLS - 1] = -corr
    ext[2] = -kappa * dec(x + 1)
    ext[3, 0] = corr
    ehi, elo = split_np(np.repeat(ext, PLANES, axis=0))
    zero = np.zeros_like(elo)
    stencil = np.concatenate([whi, whi, wlo, ehi, elo, ehi, zero], axis=0)
    edge = np.zeros((CELLS, 4))
    edge[:, 0] = dec(x)
    edge[0, 1] = 1.0
    edge[:, 2] = dec(CELLS - 1 - x)
    edge[CELLS - 1, 3] = 1.0
    edge = np.concatenate([edge[:64], edge[CELLS - 64 :]], axis=0)
    edge = np.concatenate([np.repeat(edge, PLANES, axis=1), np.zeros((128, 64))], axis=1)
    ghi, glo = split_np(edge)
    return stencil, np.concatenate([ghi, ghi, glo], axis=0)


def halves(x):
    hi = x.astype(BF16)
    return hi, (x - hi.astype(F32)).astype(BF16)


def lanes(shape):
    return lax.broadcasted_iota(jnp.int32, shape, len(shape) - 1)


def sublanes(shape):
    return lax.broadcasted_iota(jnp.int32, shape, len(shape) - 2)


def edge_kernel(c_hbm, w_hbm, lower_hbm, pivot_hbm, left_ref, right_ref, c_ref, rise_ref, fall_ref, unit_ref, w_ref, lower_ref, pivot_ref, sem):
    small = [
        pltpu.make_async_copy(a, b, sem.at[i])
        for i, (a, b) in enumerate([(lower_hbm, lower_ref), (pivot_hbm, pivot_ref), (w_hbm, w_ref)])
    ]
    big = [
        [
            pltpu.make_async_copy(c_hbm.at[f, :, t, h], c_ref.at[f, t, h], sem.at[3 + (f * 4 + t) * 2 + h])
            for t in range(4)
            for h in range(2)
        ]
        for f in range(FIELDS)
    ]
    for copy in small + sum(big, []):
        copy.start()
    small[0].wait()
    small[1].wait()
    weights(lower_ref, pivot_ref, rise_ref, fall_ref, unit_ref)
    small[2].wait()
    w = w_ref[...]
    plane, lane = lanes((8, 128)) % 16, lanes((8, 128)) // 32
    for f in range(FIELDS):
        for copy in big[f]:
            copy.wait()
        ends = [c_ref[f, :, h].reshape(PLANES * ROWS, 128) for h in range(2)]
        hi, lo = halves(jnp.where(lanes((PLANES * ROWS, 128)) < 64, ends[0], ends[1]))
        sums = jnp.dot(jnp.concatenate([hi, lo, hi], axis=1), w, preferred_element_type=F32)
        own = []
        for t in range(4):
            part = sums[t * 128 : t * 128 + 8]
            for p in range(1, PLANES):
                part = jnp.where(plane == p, sums[t * 128 + p * 8 : t * 128 + p * 8 + 8], part)
            own.append(part)
        left = own[0]
        right = pltpu.roll(own[0], 96, 1)
        for q in range(1, 4):
            part = own[q]
            left = jnp.where(lane == q, pltpu.roll(part, 32 * q, 1), left)
            right = jnp.where(lane == q, pltpu.roll(part, (32 * q + 96) % 128, 1) if q != 1 else part, right)
        left_ref[f] = left
        right_ref[f] = right


def load_row(ref, f, t, s):
    return jnp.concatenate([ref[f, pl.ds(t * 256 + h * 128 + s, PLANES, stride=8), :] for h in range(2)], 1)


def full(ref, j, f):
    v = ref[pl.ds(j * 8 + f, 8, stride=0), :]
    return jnp.concatenate([jnp.concatenate([v, v], 0)] * 2, 1)


def spread_rows(value, out_ref):
    for j in range(ROWS):
        out_ref[j * 8 : j * 8 + FIELDS, :] = jnp.broadcast_to(value[:, j : j + 1], (FIELDS, 128))


def weights(lower_ref, pivot_ref, rise_ref, fall_ref, unit_ref):
    low, piv = lower_ref[...], 1.0 / pivot_ref[...]
    wide = lambda v, j: jnp.broadcast_to(v[:, j : j + 1], (FIELDS, 128))
    entry = jnp.ones((FIELDS, 128), F32)
    direct, spread = [], jnp.zeros((FIELDS, 128), F32)
    for j in range(ROWS):
        direct.append(entry * wide(piv, j))
        spread = spread + entry * direct[j]
        entry = entry * wide(low, j)
    leave, first = None, None
    for j in reversed(range(ROWS)):
        l = wide(low, j)
        leave = l if leave is None else l * leave
        first = direct[j] if first is None else direct[j] + l * first
        rise_ref[j * 8 : j * 8 + FIELDS, :] = leave
        fall_ref[j * 8 : j * 8 + FIELDS, :] = first
    unit_ref[0, :FIELDS, :] = entry
    unit_ref[1, :FIELDS, :] = spread


def sums_kernel(c_ref, rise_ref, fall_ref, lower_ref, pivot_ref, speed_ref, out_ref, low_ref, inv_ref, sp_ref):
    spread_rows(lower_ref[...], low_ref)
    spread_rows(1.0 / pivot_ref[...], inv_ref)
    spread_rows(speed_ref[...], sp_ref)
    for f in range(FIELDS):
        up = jnp.zeros((PLANES, CELLS), F32)
        down = jnp.zeros((PLANES, CELLS), F32)
        for j in range(ROWS):
            v = load_row(c_ref, f, j // 8, j % 8)
            up = up + full(rise_ref, j, f) * v
            down = down + full(fall_ref, j, f) * v
        for h in range(2):
            for q in range(2):
                base = (16 * h + 8 * q) * 16 + f
                out_ref[pl.ds(base, 8, stride=16), :] = up[8 * q : 8 * q + 8, 128 * h : 128 * h + 128]
                out_ref[pl.ds(base + 8, 8, stride=16), :] = down[8 * q : 8 * q + 8, 128 * h : 128 * h + 128]


def merge_kernel(main_ref, rise_ref, fall_ref, unit_ref, left_ref, right_ref, out_ref, ext_ref):
    lane = lanes((8, 128))
    ups, downs = [], []
    for f in range(FIELDS):
        up = jnp.zeros((8, 128), F32)
        down = jnp.zeros((8, 128), F32)
        from_left, from_right = left_ref[f], right_ref[f]
        for q in range(4):
            r = pltpu.roll(from_right, (128 - 32 * q) % 128, 1) if q else from_right
            l = pltpu.roll(from_left, (128 - 32 * q + 32) % 128, 1) if q != 1 else from_left
            v = jnp.where(lane < 32, r, l)
            v = jnp.where(lane < 64, v, pltpu.roll(v, 64, 1))
            ext_ref[pl.ds(64 * q + f, 8, stride=8), :] = v
            up = up + rise_ref[pl.ds(64 * q + f, 8, stride=8), :] * v
            down = down + fall_ref[pl.ds(64 * q + f, 8, stride=8), :] * v
        ups.append(jnp.sum(up, axis=0, keepdims=True))
        downs.append(jnp.sum(down, axis=0, keepdims=True))
    row = sublanes((FIELDS, 128))
    lane5 = lanes((FIELDS, 128))
    coef = jnp.where(lane5 == 64 + row, unit_ref[0, :FIELDS, :], 0.0)
    coef = jnp.where(lane5 == 72 + row, unit_ref[1, :FIELDS, :], coef)
    coef = jnp.sum(coef, axis=0, keepdims=True)
    lane1 = lanes((1, 128))
    sub = sublanes((8, 128))

    def pack(v, last):
        rows = [jnp.where(lane1 < 64, v[0], v[1]), jnp.where(lane1 < 64, v[2], v[3]), jnp.where(lane1 < 64, v[4], last)]
        return jnp.where(sub == 5, rows[0], jnp.where(sub == 6, rows[1], rows[2]))

    tail_up, tail_down = pack(ups, coef), pack(downs, jnp.zeros((1, 128), F32))
    for k in range(WALLS):
        out_ref[k, :8, :] = jnp.where(sub < 5, main_ref[16 * k : 16 * k + 8, :], tail_up)
        out_ref[k, 8:, :] = jnp.where(sub < 5, main_ref[16 * k + 8 : 16 * k + 16, :], tail_down)


def carry_kernel(in_ref, out_ref, seam_ref, through_ref, crest_ref):
    me = lax.axis_index("wall")
    sub, lane = sublanes((8, 128)), lanes((8, 128))
    low_field = jnp.where(sub < 5, sub, 2 * (sub - 5))
    high_field = jnp.where(sub < 5, sub, jnp.where(sub < 7, 2 * (sub - 5) + 1, 4))

    def pick(row, at):
        lo = jnp.sum(jnp.where(lane == at + low_field, row, 0.0), axis=1, keepdims=True)
        hi = jnp.sum(jnp.where(lane == at + high_field, row, 0.0), axis=1, keepdims=True)
        return jnp.where(lane < 64, lo, hi)

    run, mine = jnp.zeros((8, 128), F32), jnp.zeros((8, 128), F32)
    for d in range(WALLS):
        row = jnp.broadcast_to(in_ref[d, 7:8, :], (8, 128))
        through, spread = pick(row, 64), pick(row, 72)
        through_ref[d] = through
        out_ref[12 * d : 12 * d + 5, :] = run[:5]
        mine = jnp.where(me == d, run, mine)
        crest_ref[d] = in_ref[d, 8:, :] + spread * run
        run = through * run + in_ref[d, :8, :]
    seam_ref[0] = mine
    run, mine = jnp.zeros((8, 128), F32), jnp.zeros((8, 128), F32)
    for d in reversed(range(WALLS)):
        out_ref[12 * d + 5 : 12 * d + 10, :] = run[:5]
        out_ref[12 * d + 10 : 12 * d + 12, :] = jnp.zeros((2, 128), F32)
        mine = jnp.where(me == d, run, mine)
        run = through_ref[d] * run + crest_ref[d]
    seam_ref[1] = mine


def final_kernel(
    c_ref, ret_ref, seam_ref, low_ref, inv_ref, sp_ref, ext_ref, w_ref, o_ref, fe_ref, fl_ref, sc_ref, lhs_ref, res_ref, sem
):
    sub, lane = sublanes((8, 128)), lanes((8, 128))

    def unpack(tile):
        turned = pltpu.roll(tile, 64, 1)
        a, b = jnp.where(lane < 64, tile, turned), jnp.where(lane < 64, turned, tile)
        rows = [a[5:6], b[5:6], a[6:7], b[6:7], a[7:8]]
        out = jnp.broadcast_to(rows[4], (8, 128))
        for f in range(4):
            out = jnp.where(sub == f, rows[f], out)
        return jnp.where(sub < FIELDS, out, 0.0)

    run = unpack(seam_ref[0])
    for j in range(ROWS):
        run = ext_ref[j * 8 : j * 8 + 8, :] + run
        fe_ref[j * 8 : j * 8 + 8, :] = run * inv_ref[j * 8 : j * 8 + 8, :]
        run = run * low_ref[j * 8 : j * 8 + 8, :]
    run = unpack(seam_ref[1])
    for j in reversed(range(ROWS)):
        run = fe_ref[j * 8 : j * 8 + 8, :] + low_ref[j * 8 : j * 8 + 8, :] * run
        fe_ref[j * 8 : j * 8 + 8, :] = run * sp_ref[j * 8 : j * 8 + 8, :]

    for j in range(ROWS):
        hi, lo = halves(fe_ref[j * 8 : j * 8 + 8, :])
        fe_ref[j * 8 : j * 8 + 8, :] = hi.astype(F32)
        fl_ref[j * 8 : j * 8 + 8, :] = lo.astype(F32)

    mine = lanes((PLANES, 128)) % 16 == sublanes((PLANES, 128))
    w = w_ref[...]

    def carry(f, shift):
        parts = [[ret_ref[pl.ds((16 * h + 8 * q) * 12 + f + shift, 8, stride=12), :] for h in range(2)] for q in range(2)]
        return jnp.concatenate([jnp.concatenate(p, 1) for p in parts], 0)

    def planes(ref, j, f):
        v = ref[pl.ds(j * 8 + f, 8, stride=0), :]
        return jnp.where(mine, jnp.concatenate([v, v], 0), 0.0).astype(BF16)

    def rise(i, run):
        run = list(run)
        t = i // 4
        for u in range(2):
            s = (i % 4) * 2 + u
            j = i * 2 + u
            for f in range(FIELDS):
                now = load_row(c_ref, f, t, s) + run[f]
                sc_ref[f, pl.ds(pl.multiple_of(i * 32, 32) + u * 16, 16), :] = now * full(inv_ref, j, f)
                run[f] = now * full(low_ref, j, f)
        return tuple(run)

    lax.fori_loop(0, 16, rise, tuple(carry(f, 0) for f in range(FIELDS)))
    run = [carry(f, 5) for f in range(FIELDS)]
    copies = []
    for t in reversed(range(4)):
        for j in reversed(range(8 * t, 8 * t + 8)):
            for f in range(FIELDS):
                run[f] = sc_ref[f, j * 16 : j * 16 + 16, :] + full(low_ref, j, f) * run[f]
                sc_ref[f, j * 16 : j * 16 + 16, :] = run[f]
                hi, lo = halves(run[f] * full(sp_ref, j, f))
                at = f * 128 + (j % 8) * 16
                lhs_ref[t % 2, at : at + 16, :] = jnp.concatenate([hi, lo, hi, planes(fe_ref, j, f), planes(fl_ref, j, f)], 1)
        out = jnp.dot(lhs_ref[t % 2], w, preferred_element_type=F32)
        for f in range(FIELDS):
            for s in range(8):
                j, at = 8 * t + s, f * 128 + s * 16
                value = out[at : at + 16] + sc_ref[f, j * 16 : j * 16 + 16, :]
                for h in range(2):
                    res_ref[t, h, pl.ds(f * 128 + s, PLANES, stride=8), :] = value[:, 128 * h : 128 * h + 128]
        for h in range(2):
            source = res_ref.at[t, h].reshape(FIELDS * PLANES, 8, 128)
            copies.append(pltpu.make_async_copy(source, o_ref.at[:, t, h], sem.at[2 * t + h]))
            copies[-1].start()
    for copy in copies:
        copy.wait()


def params():
    return pltpu.CompilerParams(vmem_limit_bytes=24 * 1024 * 1024)


VM = pl.BlockSpec(memory_space=pltpu.VMEM)


def local(cotangent, lower, pivot, speed):
    stencil, edge = tables()
    sds = jax.ShapeDtypeStruct
    flat = cotangent.reshape(FIELDS, PLANES, 4, 8, 2, 128).transpose(0, 1, 2, 4, 3, 5)
    rows = sds((ROWS * 8, 128), F32)
    left, right, cells, rise, fall, unit = pl.pallas_call(
        edge_kernel,
        out_shape=[sds((FIELDS, 8, 128), F32)] * 2 + [sds((FIELDS, 4, 2, PLANES, 8, 128), F32), rows, rows, sds((2, 8, 128), F32)],
        in_specs=[pl.BlockSpec(memory_space=pltpu.HBM)] * 4,
        out_specs=[VM] * 6,
        scratch_shapes=[
            pltpu.VMEM((384, 128), BF16),
            pltpu.VMEM((FIELDS, ROWS), F32),
            pltpu.VMEM((FIELDS, ROWS), F32),
            pltpu.SemaphoreType.DMA((8 * FIELDS + 3,)),
        ],
        compiler_params=params(),
        name="edge",
    )(*[pltpu.with_memory_space_constraint(v, pltpu.HBM) for v in (flat, jnp.asarray(edge), lower, pivot)])
    cells = cells.reshape(FIELDS, 1024, 128)
    count = lax.axis_size("stream")
    from_left = lax.ppermute(right, "stream", [(i, (i + 1) % count) for i in range(count)])
    from_right = lax.ppermute(left, "stream", [((i + 1) % count, i) for i in range(count)])
    main, low, inv, sp = pl.pallas_call(
        sums_kernel,
        out_shape=[sds((WALLS * 16, 128), F32), rows, rows, rows],
        in_specs=[VM] * 6,
        out_specs=[VM] * 4,
        compiler_params=params(),
        cost_estimate=pl.CostEstimate(flops=4000000, bytes_accessed=2600000, transcendentals=0),
        name="sums",
    )(cells, rise, fall, lower, pivot, speed)
    send, ext = pl.pallas_call(
        merge_kernel,
        out_shape=[sds((WALLS, 16, 128), F32), rows],
        in_specs=[VM] * 6,
        out_specs=[VM] * 2,
        compiler_params=params(),
        name="merge",
    )(main, rise, fall, unit, from_left, from_right)
    got = lax.all_to_all(send, "wall", 0, 0, tiled=True)
    carries, seam = pl.pallas_call(
        carry_kernel,
        out_shape=[sds((WALLS * 12, 128), F32), sds((2, 8, 128), F32)],
        in_specs=[VM],
        out_specs=[VM] * 2,
        scratch_shapes=[pltpu.VMEM((WALLS, 8, 128), F32)] * 2,
        compiler_params=params(),
        name="carry",
    )(got)
    back = lax.all_to_all(carries.reshape(WALLS, 3, 4, 128), "wall", 0, 0, tiled=True)
    out = pl.pallas_call(
        final_kernel,
        out_shape=sds((FIELDS * PLANES, 4, 2, 8, 128), F32),
        in_specs=[VM] * 8,
        out_specs=pl.BlockSpec(memory_space=pl.ANY),
        scratch_shapes=[pltpu.VMEM((ROWS * 8, 128), F32)] * 2
        + [
            pltpu.VMEM((FIELDS, ROWS * PLANES, CELLS), F32),
            pltpu.VMEM((2, FIELDS * PLANES * 8, 1024), BF16),
            pltpu.VMEM((4, 2, FIELDS * PLANES * 8, 128), F32),
            pltpu.SemaphoreType.DMA((8,)),
        ],
        compiler_params=params(),
        name="final",
    )(cells, back.reshape(WALLS * 12, 128), seam, low, inv, sp, ext, jnp.asarray(stencil))
    return out.reshape(FIELDS, PLANES, 4, 2, 8, 128).transpose(0, 1, 2, 4, 3, 5).reshape(FIELDS, PLANES, ROWS, CELLS)


def solution(mesh):
    return jax.shard_map(
        local,
        mesh=mesh,
        in_specs=(P(None, None, "wall", "stream"), P(None, "wall"), P(None, "wall"), P(None, "wall")),
        out_specs=P(None, None, "wall", "stream"),
        check_vma=False,
    )
```

```python
import math

import jax
import jax.numpy as jnp
import ml_dtypes
import numpy as np
from jax import lax
from jax.experimental import pallas as pl
from jax.experimental.pallas import tpu as pltpu
from jax.sharding import PartitionSpec as P

F32, BF16 = jnp.float32, jnp.bfloat16
R = (math.sqrt(5.0) - 3.0) / 2.0
GAIN = 3.0 / math.sqrt(5.0)
C1 = 7.0 / 9.0
C2 = 1.0 / 36.0
FIELDS, PLANES, ROWS, CELLS, WALLS = 5, 16, 32, 256, 32


def split_np(w):
    w = np.asarray(w, np.float64)
    hi = w.astype(ml_dtypes.bfloat16)
    lo = (w - hi.astype(np.float64)).astype(ml_dtypes.bfloat16)
    return hi, lo


def tables():
    dec = lambda n: np.where(np.abs(n) % 2 == 0, 1.0, -1.0) * np.abs(R) ** np.abs(n)
    off = np.arange(CELLS)[:, None] - np.arange(CELLS)[None, :]
    tap = lambda o: GAIN * (C1 * (dec(o - 1) - dec(o + 1)) + C2 * (dec(o - 2) - dec(o + 2)))
    whi, wlo = split_np(tap(off))
    kappa = GAIN * (C1 * (1.0 / R - R) + C2 * (R**-2 - R**2))
    corr = tap(np.array(-1)) + kappa * R
    x = np.arange(CELLS)
    ext = np.zeros((4, CELLS))
    ext[0] = kappa * dec(CELLS - x)
    ext[1, CELLS - 1] = -corr
    ext[2] = -kappa * dec(x + 1)
    ext[3, 0] = corr
    ehi, elo = split_np(np.repeat(ext, PLANES, axis=0))
    zero = np.zeros_like(elo)
    stencil = np.concatenate([whi, whi, wlo, ehi, elo, ehi, zero], axis=0)
    edge = np.zeros((CELLS, 4))
    edge[:, 0] = dec(x)
    edge[0, 1] = 1.0
    edge[:, 2] = dec(CELLS - 1 - x)
    edge[CELLS - 1, 3] = 1.0
    edge = np.concatenate([edge[:64], edge[CELLS - 64 :]], axis=0)
    edge = np.concatenate([np.repeat(edge, PLANES, axis=1), np.zeros((128, 64))], axis=1)
    ghi, glo = split_np(edge)
    return stencil, np.concatenate([ghi, ghi, glo], axis=0)


def halves(x):
    hi = x.astype(BF16)
    return hi, (x - hi.astype(F32)).astype(BF16)


def lanes(shape):
    return lax.broadcasted_iota(jnp.int32, shape, len(shape) - 1)


def sublanes(shape):
    return lax.broadcasted_iota(jnp.int32, shape, len(shape) - 2)


def edge_kernel(c_hbm, w_hbm, lower_hbm, pivot_hbm, left_ref, right_ref, c_ref, rise_ref, fall_ref, gain_ref, unit_ref, w_ref, lower_ref, pivot_ref, sem):
    small = [
        pltpu.make_async_copy(a, b, sem.at[i])
        for i, (a, b) in enumerate([(lower_hbm, lower_ref), (pivot_hbm, pivot_ref), (w_hbm, w_ref)])
    ]
    big = [
        [pltpu.make_async_copy(c_hbm.at[f, p], c_ref.at[f, :, :, p], sem.at[3 + f * PLANES + p]) for p in range(PLANES)]
        for f in range(FIELDS)
    ]
    for copy in small + sum(big, []):
        copy.start()
    small[0].wait()
    small[1].wait()
    weights(lower_ref, pivot_ref, rise_ref, fall_ref, gain_ref, unit_ref)
    small[2].wait()
    w = w_ref[...]
    plane, lane = lanes((8, 128)) % 16, lanes((8, 128)) // 32
    for f in range(FIELDS):
        for copy in big[f]:
            copy.wait()
        ends = [c_ref[f, :, h].reshape(PLANES * ROWS, 128) for h in range(2)]
        hi, lo = halves(jnp.where(lanes((PLANES * ROWS, 128)) < 64, ends[0], ends[1]))
        sums = jnp.dot(jnp.concatenate([hi, lo, hi], axis=1), w, preferred_element_type=F32)
        own = []
        for t in range(4):
            part = sums[t * 128 : t * 128 + 8]
            for p in range(1, PLANES):
                part = jnp.where(plane == p, sums[t * 128 + p * 8 : t * 128 + p * 8 + 8], part)
            own.append(part)
        left = own[0]
        right = pltpu.roll(own[0], 96, 1)
        for q in range(1, 4):
            part = own[q]
            left = jnp.where(lane == q, pltpu.roll(part, 32 * q, 1), left)
            right = jnp.where(lane == q, pltpu.roll(part, (32 * q + 96) % 128, 1) if q != 1 else part, right)
        left_ref[f] = left
        right_ref[f] = right


def load_row(ref, f, t, s):
    return jnp.concatenate([ref[f, pl.ds(t * 256 + h * 128 + s, PLANES, stride=8), :] for h in range(2)], 1)


def full(ref, j, f):
    v = ref[pl.ds(j * 8 + f, 8, stride=0), :]
    return jnp.concatenate([jnp.concatenate([v, v], 0)] * 2, 1)


def spread_rows(value, out_ref):
    for j in range(ROWS):
        out_ref[j * 8 : j * 8 + FIELDS, :] = jnp.broadcast_to(value[:, j : j + 1], (FIELDS, 128))


def weights(lower_ref, pivot_ref, rise_ref, fall_ref, gain_ref, unit_ref):
    low, piv = lower_ref[...], 1.0 / pivot_ref[...]
    wide = lambda v, j: jnp.broadcast_to(v[:, j : j + 1], (FIELDS, 128))
    entry = jnp.ones((FIELDS, 128), F32)
    direct, spread = [], jnp.zeros((FIELDS, 128), F32)
    for j in range(ROWS):
        direct.append(entry * wide(piv, j))
        gain_ref[j * 8 : j * 8 + FIELDS, :] = direct[j]
        spread = spread + entry * direct[j]
        entry = entry * wide(low, j)
    leave, first = None, None
    for j in reversed(range(ROWS)):
        l = wide(low, j)
        leave = l if leave is None else l * leave
        first = direct[j] if first is None else direct[j] + l * first
        rise_ref[j * 8 : j * 8 + FIELDS, :] = leave
        fall_ref[j * 8 : j * 8 + FIELDS, :] = first
    unit_ref[0, :FIELDS, :] = entry
    unit_ref[1, :FIELDS, :] = spread


def sums_kernel(c_ref, fall_ref, lower_ref, pivot_ref, speed_ref, out_ref, base_ref, low_ref, inv_ref, sp_ref):
    spread_rows(lower_ref[...], low_ref)
    spread_rows(1.0 / pivot_ref[...], inv_ref)
    spread_rows(speed_ref[...], sp_ref)
    for f in range(FIELDS):
        run = jnp.zeros((PLANES, CELLS), F32)
        down = jnp.zeros((PLANES, CELLS), F32)
        for j in range(ROWS):
            v = load_row(c_ref, f, j // 8, j % 8)
            down = down + full(fall_ref, j, f) * v
            run = v + run
            base_ref[f, j * 16 : j * 16 + 16, :] = run * full(inv_ref, j, f)
            run = run * full(low_ref, j, f)
        for h in range(2):
            for q in range(2):
                base = (16 * h + 8 * q) * 16 + f
                out_ref[pl.ds(base, 8, stride=16), :] = run[8 * q : 8 * q + 8, 128 * h : 128 * h + 128]
                out_ref[pl.ds(base + 8, 8, stride=16), :] = down[8 * q : 8 * q + 8, 128 * h : 128 * h + 128]


def merge_kernel(main_ref, rise_ref, fall_ref, unit_ref, left_ref, right_ref, out_ref, ext_ref):
    lane = lanes((8, 128))
    ups, downs = [], []
    for f in range(FIELDS):
        up = jnp.zeros((8, 128), F32)
        down = jnp.zeros((8, 128), F32)
        from_left, from_right = left_ref[f], right_ref[f]
        for q in range(4):
            r = pltpu.roll(from_right, (128 - 32 * q) % 128, 1) if q else from_right
            l = pltpu.roll(from_left, (128 - 32 * q + 32) % 128, 1) if q != 1 else from_left
            v = jnp.where(lane < 32, r, l)
            v = jnp.where(lane < 64, v, pltpu.roll(v, 64, 1))
            ext_ref[pl.ds(64 * q + f, 8, stride=8), :] = v
            up = up + rise_ref[pl.ds(64 * q + f, 8, stride=8), :] * v
            down = down + fall_ref[pl.ds(64 * q + f, 8, stride=8), :] * v
        ups.append(jnp.sum(up, axis=0, keepdims=True))
        downs.append(jnp.sum(down, axis=0, keepdims=True))
    row = sublanes((FIELDS, 128))
    lane5 = lanes((FIELDS, 128))
    coef = jnp.where(lane5 == 64 + row, unit_ref[0, :FIELDS, :], 0.0)
    coef = jnp.where(lane5 == 72 + row, unit_ref[1, :FIELDS, :], coef)
    coef = jnp.sum(coef, axis=0, keepdims=True)
    lane1 = lanes((1, 128))
    sub = sublanes((8, 128))

    def pack(v, last):
        rows = [jnp.where(lane1 < 64, v[0], v[1]), jnp.where(lane1 < 64, v[2], v[3]), jnp.where(lane1 < 64, v[4], last)]
        return jnp.where(sub == 5, rows[0], jnp.where(sub == 6, rows[1], rows[2]))

    tail_up, tail_down = pack(ups, coef), pack(downs, jnp.zeros((1, 128), F32))
    for k in range(WALLS):
        out_ref[k, :8, :] = jnp.where(sub < 5, main_ref[16 * k : 16 * k + 8, :], tail_up)
        out_ref[k, 8:, :] = jnp.where(sub < 5, main_ref[16 * k + 8 : 16 * k + 16, :], tail_down)


def carry_kernel(in_ref, out_ref, seam_ref, through_ref, crest_ref):
    me = lax.axis_index("wall")
    sub, lane = sublanes((8, 128)), lanes((8, 128))
    low_field = jnp.where(sub < 5, sub, 2 * (sub - 5))
    high_field = jnp.where(sub < 5, sub, jnp.where(sub < 7, 2 * (sub - 5) + 1, 4))

    def pick(row, at):
        lo = jnp.sum(jnp.where(lane == at + low_field, row, 0.0), axis=1, keepdims=True)
        hi = jnp.sum(jnp.where(lane == at + high_field, row, 0.0), axis=1, keepdims=True)
        return jnp.where(lane < 64, lo, hi)

    run, mine = jnp.zeros((8, 128), F32), jnp.zeros((8, 128), F32)
    for d in range(WALLS):
        row = jnp.broadcast_to(in_ref[d, 7:8, :], (8, 128))
        through, spread = pick(row, 64), pick(row, 72)
        through_ref[d] = through
        out_ref[12 * d : 12 * d + 5, :] = run[:5]
        mine = jnp.where(me == d, run, mine)
        crest_ref[d] = in_ref[d, 8:, :] + spread * run
        run = through * run + in_ref[d, :8, :]
    seam_ref[0] = mine
    run, mine = jnp.zeros((8, 128), F32), jnp.zeros((8, 128), F32)
    for d in reversed(range(WALLS)):
        out_ref[12 * d + 5 : 12 * d + 10, :] = run[:5]
        out_ref[12 * d + 10 : 12 * d + 12, :] = jnp.zeros((2, 128), F32)
        mine = jnp.where(me == d, run, mine)
        run = through_ref[d] * run + crest_ref[d]
    seam_ref[1] = mine


def final_kernel(
    base_ref, ret_ref, seam_ref, low_ref, inv_ref, gain_ref, sp_ref, ext_ref, w_ref, o_ref, fe_ref, fl_ref, in_ref, sc_ref, lhs_ref, res_ref, sem
):
    sub, lane = sublanes((8, 128)), lanes((8, 128))

    def unpack(tile):
        turned = pltpu.roll(tile, 64, 1)
        a, b = jnp.where(lane < 64, tile, turned), jnp.where(lane < 64, turned, tile)
        rows = [a[5:6], b[5:6], a[6:7], b[6:7], a[7:8]]
        out = jnp.broadcast_to(rows[4], (8, 128))
        for f in range(4):
            out = jnp.where(sub == f, rows[f], out)
        return jnp.where(sub < FIELDS, out, 0.0)

    run = unpack(seam_ref[0])
    for j in range(ROWS):
        run = ext_ref[j * 8 : j * 8 + 8, :] + run
        fe_ref[j * 8 : j * 8 + 8, :] = run * inv_ref[j * 8 : j * 8 + 8, :]
        run = run * low_ref[j * 8 : j * 8 + 8, :]
    run = unpack(seam_ref[1])
    for j in reversed(range(ROWS)):
        run = fe_ref[j * 8 : j * 8 + 8, :] + low_ref[j * 8 : j * 8 + 8, :] * run
        fe_ref[j * 8 : j * 8 + 8, :] = run * sp_ref[j * 8 : j * 8 + 8, :]

    for j in range(ROWS):
        hi, lo = halves(fe_ref[j * 8 : j * 8 + 8, :])
        fe_ref[j * 8 : j * 8 + 8, :] = hi.astype(F32)
        fl_ref[j * 8 : j * 8 + 8, :] = lo.astype(F32)

    mine = lanes((PLANES, 128)) % 16 == sublanes((PLANES, 128))
    w = w_ref[...]

    def carry(f, shift):
        parts = [[ret_ref[pl.ds((16 * h + 8 * q) * 12 + f + shift, 8, stride=12), :] for h in range(2)] for q in range(2)]
        return jnp.concatenate([jnp.concatenate(p, 1) for p in parts], 0)

    def planes(ref, j, f):
        v = ref[pl.ds(j * 8 + f, 8, stride=0), :]
        return jnp.where(mine, jnp.concatenate([v, v], 0), 0.0).astype(BF16)

    for f in range(FIELDS):
        in_ref[f] = carry(f, 0)
    run = [carry(f, 5) for f in range(FIELDS)]
    copies = []
    for t in reversed(range(4)):
        for j in reversed(range(8 * t, 8 * t + 8)):
            for f in range(FIELDS):
                scaled = base_ref[f, j * 16 : j * 16 + 16, :] + full(gain_ref, j, f) * in_ref[f]
                run[f] = scaled + full(low_ref, j, f) * run[f]
                sc_ref[f, j * 16 : j * 16 + 16, :] = run[f]
                hi, lo = halves(run[f] * full(sp_ref, j, f))
                at = f * 128 + (j % 8) * 16
                lhs_ref[t, at : at + 16, :] = jnp.concatenate([hi, lo, hi, planes(fe_ref, j, f), planes(fl_ref, j, f)], 1)
        out = jnp.dot(lhs_ref[t], w, preferred_element_type=F32)
        for f in range(FIELDS):
            for s in range(8):
                j, at = 8 * t + s, f * 128 + s * 16
                value = out[at : at + 16] + sc_ref[f, j * 16 : j * 16 + 16, :]
                for h in range(2):
                    res_ref[t, h, pl.ds(f * 128 + s, PLANES, stride=8), :] = value[:, 128 * h : 128 * h + 128]
        for h in range(2):
            source = res_ref.at[t, h].reshape(FIELDS * PLANES, 8, 128)
            copies.append(pltpu.make_async_copy(source, o_ref.at[:, t, h], sem.at[2 * t + h]))
            copies[-1].start()
    for copy in copies:
        copy.wait()


def params():
    return pltpu.CompilerParams(vmem_limit_bytes=24 * 1024 * 1024)


VM = pl.BlockSpec(memory_space=pltpu.VMEM)


def local(cotangent, lower, pivot, speed):
    stencil, edge = tables()
    sds = jax.ShapeDtypeStruct
    flat = cotangent.reshape(FIELDS, PLANES, 4, 8, 2, 128).transpose(0, 1, 2, 4, 3, 5)
    rows = sds((ROWS * 8 + 8, 128), F32)
    left, right, cells, rise, fall, gain, unit = pl.pallas_call(
        edge_kernel,
        out_shape=[sds((FIELDS, 8, 128), F32)] * 2 + [sds((FIELDS, 4, 2, PLANES, 8, 128), F32), rows, rows, rows, sds((2, 8, 128), F32)],
        in_specs=[pl.BlockSpec(memory_space=pltpu.HBM)] * 4,
        out_specs=[VM] * 7,
        scratch_shapes=[
            pltpu.VMEM((384, 128), BF16),
            pltpu.VMEM((FIELDS, ROWS), F32),
            pltpu.VMEM((FIELDS, ROWS), F32),
            pltpu.SemaphoreType.DMA((PLANES * FIELDS + 3,)),
        ],
        compiler_params=params(),
        name="edge",
    )(*[pltpu.with_memory_space_constraint(v, pltpu.HBM) for v in (flat, jnp.asarray(edge), lower, pivot)])
    cells = cells.reshape(FIELDS, 1024, 128)
    count = lax.axis_size("stream")
    from_left = lax.ppermute(right, "stream", [(i, (i + 1) % count) for i in range(count)])
    from_right = lax.ppermute(left, "stream", [((i + 1) % count, i) for i in range(count)])
    main, base, low, inv, sp = pl.pallas_call(
        sums_kernel,
        out_shape=[sds((WALLS * 16, 128), F32), sds((FIELDS, ROWS * PLANES, CELLS), F32), rows, rows, rows],
        in_specs=[VM] * 5,
        out_specs=[VM] * 5,
        compiler_params=params(),
        cost_estimate=pl.CostEstimate(flops=4000000, bytes_accessed=2600000, transcendentals=0),
        name="sums",
    )(cells, fall, lower, pivot, speed)
    send, ext = pl.pallas_call(
        merge_kernel,
        out_shape=[sds((WALLS, 16, 128), F32), rows],
        in_specs=[VM] * 6,
        out_specs=[VM] * 2,
        compiler_params=params(),
        name="merge",
    )(main, rise, fall, unit, from_left, from_right)
    got = lax.all_to_all(send, "wall", 0, 0, tiled=True)
    carries, seam = pl.pallas_call(
        carry_kernel,
        out_shape=[sds((WALLS * 12, 128), F32), sds((2, 8, 128), F32)],
        in_specs=[VM],
        out_specs=[VM] * 2,
        scratch_shapes=[pltpu.VMEM((WALLS, 8, 128), F32)] * 2,
        compiler_params=params(),
        name="carry",
    )(got)
    back = lax.all_to_all(carries.reshape(WALLS, 3, 4, 128), "wall", 0, 0, tiled=True)
    out = pl.pallas_call(
        final_kernel,
        out_shape=sds((FIELDS * PLANES, 4, 2, 8, 128), F32),
        in_specs=[VM] * 9,
        out_specs=pl.BlockSpec(memory_space=pl.ANY),
        scratch_shapes=[pltpu.VMEM((ROWS * 8 + 8, 128), F32)] * 2
        + [
            pltpu.VMEM((FIELDS, PLANES, CELLS), F32),
            pltpu.VMEM((FIELDS, ROWS * PLANES, CELLS), F32),
            pltpu.VMEM((4, FIELDS * PLANES * 8, 1024), BF16),
            pltpu.VMEM((4, 2, FIELDS * PLANES * 8, 128), F32),
            pltpu.SemaphoreType.DMA((8,)),
        ],
        compiler_params=params(),
        name="final",
    )(base, back.reshape(WALLS * 12, 128), seam, low, inv, gain, sp, ext, jnp.asarray(stencil))
    return out.reshape(FIELDS, PLANES, 4, 2, 8, 128).transpose(0, 1, 2, 4, 3, 5).reshape(FIELDS, PLANES, ROWS, CELLS)


def solution(mesh):
    return jax.shard_map(
        local,
        mesh=mesh,
        in_specs=(P(None, None, "wall", "stream"), P(None, "wall"), P(None, "wall"), P(None, "wall")),
        out_specs=P(None, None, "wall", "stream"),
        check_vma=False,
    )
```

```python
import math

import jax
import jax.numpy as jnp
import ml_dtypes
import numpy as np
from jax import lax
from jax.experimental import pallas as pl
from jax.experimental.pallas import tpu as pltpu
from jax.sharding import PartitionSpec as P

F32, BF16 = jnp.float32, jnp.bfloat16
R = (math.sqrt(5.0) - 3.0) / 2.0
GAIN = 3.0 / math.sqrt(5.0)
C1 = 7.0 / 9.0
C2 = 1.0 / 36.0
FIELDS, PLANES, ROWS, CELLS, WALLS = 5, 16, 32, 256, 32


def split_np(w):
    w = np.asarray(w, np.float64)
    hi = w.astype(ml_dtypes.bfloat16)
    lo = (w - hi.astype(np.float64)).astype(ml_dtypes.bfloat16)
    return hi, lo


def tables():
    dec = lambda n: np.where(np.abs(n) % 2 == 0, 1.0, -1.0) * np.abs(R) ** np.abs(n)
    off = np.arange(CELLS)[:, None] - np.arange(CELLS)[None, :]
    tap = lambda o: GAIN * (C1 * (dec(o - 1) - dec(o + 1)) + C2 * (dec(o - 2) - dec(o + 2)))
    whi, wlo = split_np(tap(off))
    kappa = GAIN * (C1 * (1.0 / R - R) + C2 * (R**-2 - R**2))
    corr = tap(np.array(-1)) + kappa * R
    x = np.arange(CELLS)
    ext = np.zeros((4, CELLS))
    ext[0] = kappa * dec(CELLS - x)
    ext[1, CELLS - 1] = -corr
    ext[2] = -kappa * dec(x + 1)
    ext[3, 0] = corr
    ehi, elo = split_np(np.repeat(ext, PLANES, axis=0))
    zero = np.zeros_like(elo)
    stencil = np.concatenate([whi, whi, wlo, ehi, elo, ehi, zero], axis=0)
    edge = np.zeros((CELLS, 4))
    edge[:, 0] = dec(x)
    edge[0, 1] = 1.0
    edge[:, 2] = dec(CELLS - 1 - x)
    edge[CELLS - 1, 3] = 1.0
    edge = np.concatenate([edge[:64], edge[CELLS - 64 :]], axis=0)
    edge = np.concatenate([np.repeat(edge, PLANES, axis=1), np.zeros((128, 64))], axis=1)
    ghi, glo = split_np(edge)
    return stencil, np.concatenate([ghi, ghi, glo], axis=0)


def halves(x):
    hi = x.astype(BF16)
    return hi, (x - hi.astype(F32)).astype(BF16)


def lanes(shape):
    return lax.broadcasted_iota(jnp.int32, shape, len(shape) - 1)


def sublanes(shape):
    return lax.broadcasted_iota(jnp.int32, shape, len(shape) - 2)


def edge_kernel(c_hbm, w_hbm, lower_hbm, pivot_hbm, left_ref, right_ref, c_ref, rise_ref, fall_ref, gain_ref, unit_ref, w_ref, lower_ref, pivot_ref, sem):
    small = [
        pltpu.make_async_copy(a, b, sem.at[i])
        for i, (a, b) in enumerate([(lower_hbm, lower_ref), (pivot_hbm, pivot_ref), (w_hbm, w_ref)])
    ]
    big = [
        [
            pltpu.make_async_copy(c_hbm.at[f, :, t, h], c_ref.at[f, t, h], sem.at[3 + (f * 4 + t) * 2 + h])
            for t in range(4)
            for h in range(2)
        ]
        for f in range(FIELDS)
    ]
    for copy in [small[2]] + big[0] + big[1] + small[:2] + sum(big[2:], []):
        copy.start()
    small[2].wait()
    w = w_ref[...]
    plane, lane = lanes((8, 128)) % 16, lanes((8, 128)) // 32

    def edges(f):
        ends = [c_ref[f, :, h].reshape(PLANES * ROWS, 128) for h in range(2)]
        hi, lo = halves(jnp.where(lanes((PLANES * ROWS, 128)) < 64, ends[0], ends[1]))
        sums = jnp.dot(jnp.concatenate([hi, lo, hi], axis=1), w, preferred_element_type=F32)
        own = []
        for t in range(4):
            part = sums[t * 128 : t * 128 + 8]
            for p in range(1, PLANES):
                part = jnp.where(plane == p, sums[t * 128 + p * 8 : t * 128 + p * 8 + 8], part)
            own.append(part)
        left = own[0]
        right = pltpu.roll(own[0], 96, 1)
        for q in range(1, 4):
            part = own[q]
            left = jnp.where(lane == q, pltpu.roll(part, 32 * q, 1), left)
            right = jnp.where(lane == q, pltpu.roll(part, (32 * q + 96) % 128, 1) if q != 1 else part, right)
        left_ref[f] = left
        right_ref[f] = right

    for copy in big[0] + big[1]:
        copy.wait()
    edges(0)
    edges(1)
    for copy in small[:2] + sum(big[2:], []):
        copy.wait()
    weights(lower_ref, pivot_ref, rise_ref, fall_ref, gain_ref, unit_ref)
    for f in range(2, FIELDS):
        edges(f)


def load_row(ref, f, t, s):
    return jnp.concatenate([ref[f, pl.ds(t * 256 + h * 128 + s, PLANES, stride=8), :] for h in range(2)], 1)


def full(ref, j, f):
    v = ref[pl.ds(j * 8 + f, 8, stride=0), :]
    return jnp.concatenate([jnp.concatenate([v, v], 0)] * 2, 1)


def spread_rows(value, out_ref):
    for j in range(ROWS):
        out_ref[j * 8 : j * 8 + FIELDS, :] = jnp.broadcast_to(value[:, j : j + 1], (FIELDS, 128))


def weights(lower_ref, pivot_ref, rise_ref, fall_ref, gain_ref, unit_ref):
    low, piv = lower_ref[...], 1.0 / pivot_ref[...]
    wide = lambda v, j: jnp.broadcast_to(v[:, j : j + 1], (FIELDS, 128))
    entry = jnp.ones((FIELDS, 128), F32)
    direct, spread = [], jnp.zeros((FIELDS, 128), F32)
    for j in range(ROWS):
        direct.append(entry * wide(piv, j))
        gain_ref[j * 8 : j * 8 + FIELDS, :] = direct[j]
        spread = spread + entry * direct[j]
        entry = entry * wide(low, j)
    leave, first = None, None
    for j in reversed(range(ROWS)):
        l = wide(low, j)
        leave = l if leave is None else l * leave
        first = direct[j] if first is None else direct[j] + l * first
        rise_ref[j * 8 : j * 8 + FIELDS, :] = leave
        fall_ref[j * 8 : j * 8 + FIELDS, :] = first
    unit_ref[0, :FIELDS, :] = entry
    unit_ref[1, :FIELDS, :] = spread


def sums_kernel(c_ref, fall_ref, lower_ref, pivot_ref, speed_ref, out_ref, base_ref, low_ref, inv_ref, sp_ref):
    spread_rows(lower_ref[...], low_ref)
    spread_rows(1.0 / pivot_ref[...], inv_ref)
    spread_rows(speed_ref[...], sp_ref)
    for f in range(FIELDS):
        run = jnp.zeros((PLANES, CELLS), F32)
        down = jnp.zeros((PLANES, CELLS), F32)
        for j in range(ROWS):
            v = load_row(c_ref, f, j // 8, j % 8)
            down = down + full(fall_ref, j, f) * v
            run = v + run
            base_ref[f, j * 16 : j * 16 + 16, :] = run * full(inv_ref, j, f)
            run = run * full(low_ref, j, f)
        for h in range(2):
            for q in range(2):
                base = (16 * h + 8 * q) * 16 + f
                out_ref[pl.ds(base, 8, stride=16), :] = run[8 * q : 8 * q + 8, 128 * h : 128 * h + 128]
                out_ref[pl.ds(base + 8, 8, stride=16), :] = down[8 * q : 8 * q + 8, 128 * h : 128 * h + 128]


def merge_kernel(main_ref, rise_ref, fall_ref, unit_ref, left_ref, right_ref, out_ref, ext_ref):
    lane = lanes((8, 128))
    ups, downs = [], []
    for f in range(FIELDS):
        up = jnp.zeros((8, 128), F32)
        down = jnp.zeros((8, 128), F32)
        from_left, from_right = left_ref[f], right_ref[f]
        for q in range(4):
            r = pltpu.roll(from_right, (128 - 32 * q) % 128, 1) if q else from_right
            l = pltpu.roll(from_left, (128 - 32 * q + 32) % 128, 1) if q != 1 else from_left
            v = jnp.where(lane < 32, r, l)
            v = jnp.where(lane < 64, v, pltpu.roll(v, 64, 1))
            ext_ref[pl.ds(64 * q + f, 8, stride=8), :] = v
            up = up + rise_ref[pl.ds(64 * q + f, 8, stride=8), :] * v
            down = down + fall_ref[pl.ds(64 * q + f, 8, stride=8), :] * v
        ups.append(jnp.sum(up, axis=0, keepdims=True))
        downs.append(jnp.sum(down, axis=0, keepdims=True))
    row = sublanes((FIELDS, 128))
    lane5 = lanes((FIELDS, 128))
    coef = jnp.where(lane5 == 64 + row, unit_ref[0, :FIELDS, :], 0.0)
    coef = jnp.where(lane5 == 72 + row, unit_ref[1, :FIELDS, :], coef)
    coef = jnp.sum(coef, axis=0, keepdims=True)
    lane1 = lanes((1, 128))
    sub = sublanes((8, 128))

    def pack(v, last):
        rows = [jnp.where(lane1 < 64, v[0], v[1]), jnp.where(lane1 < 64, v[2], v[3]), jnp.where(lane1 < 64, v[4], last)]
        return jnp.where(sub == 5, rows[0], jnp.where(sub == 6, rows[1], rows[2]))

    tail_up, tail_down = pack(ups, coef), pack(downs, jnp.zeros((1, 128), F32))
    for k in range(WALLS):
        out_ref[k, :8, :] = jnp.where(sub < 5, main_ref[16 * k : 16 * k + 8, :], tail_up)
        out_ref[k, 8:, :] = jnp.where(sub < 5, main_ref[16 * k + 8 : 16 * k + 16, :], tail_down)


def carry_kernel(in_ref, out_ref, seam_ref, through_ref, crest_ref):
    me = lax.axis_index("wall")
    sub, lane = sublanes((8, 128)), lanes((8, 128))
    low_field = jnp.where(sub < 5, sub, 2 * (sub - 5))
    high_field = jnp.where(sub < 5, sub, jnp.where(sub < 7, 2 * (sub - 5) + 1, 4))

    def pick(row, at):
        lo = jnp.sum(jnp.where(lane == at + low_field, row, 0.0), axis=1, keepdims=True)
        hi = jnp.sum(jnp.where(lane == at + high_field, row, 0.0), axis=1, keepdims=True)
        return jnp.where(lane < 64, lo, hi)

    run, mine = jnp.zeros((8, 128), F32), jnp.zeros((8, 128), F32)
    for d in range(WALLS):
        row = jnp.broadcast_to(in_ref[d, 7:8, :], (8, 128))
        through, spread = pick(row, 64), pick(row, 72)
        through_ref[d] = through
        out_ref[12 * d : 12 * d + 5, :] = run[:5]
        mine = jnp.where(me == d, run, mine)
        crest_ref[d] = in_ref[d, 8:, :] + spread * run
        run = through * run + in_ref[d, :8, :]
    seam_ref[0] = mine
    run, mine = jnp.zeros((8, 128), F32), jnp.zeros((8, 128), F32)
    for d in reversed(range(WALLS)):
        out_ref[12 * d + 5 : 12 * d + 10, :] = run[:5]
        out_ref[12 * d + 10 : 12 * d + 12, :] = jnp.zeros((2, 128), F32)
        mine = jnp.where(me == d, run, mine)
        run = through_ref[d] * run + crest_ref[d]
    seam_ref[1] = mine


def final_kernel(
    base_ref, ret_ref, seam_ref, low_ref, inv_ref, gain_ref, sp_ref, ext_ref, w_ref, o_ref, fe_ref, fl_ref, in_ref, sc_ref, lhs_ref, res_ref, sem
):
    sub, lane = sublanes((8, 128)), lanes((8, 128))

    def unpack(tile):
        turned = pltpu.roll(tile, 64, 1)
        a, b = jnp.where(lane < 64, tile, turned), jnp.where(lane < 64, turned, tile)
        rows = [a[5:6], b[5:6], a[6:7], b[6:7], a[7:8]]
        out = jnp.broadcast_to(rows[4], (8, 128))
        for f in range(4):
            out = jnp.where(sub == f, rows[f], out)
        return jnp.where(sub < FIELDS, out, 0.0)

    run = unpack(seam_ref[0])
    for j in range(ROWS):
        run = ext_ref[j * 8 : j * 8 + 8, :] + run
        fe_ref[j * 8 : j * 8 + 8, :] = run * inv_ref[j * 8 : j * 8 + 8, :]
        run = run * low_ref[j * 8 : j * 8 + 8, :]
    run = unpack(seam_ref[1])
    for j in reversed(range(ROWS)):
        run = fe_ref[j * 8 : j * 8 + 8, :] + low_ref[j * 8 : j * 8 + 8, :] * run
        fe_ref[j * 8 : j * 8 + 8, :] = run * sp_ref[j * 8 : j * 8 + 8, :]

    for j in range(ROWS):
        hi, lo = halves(fe_ref[j * 8 : j * 8 + 8, :])
        fe_ref[j * 8 : j * 8 + 8, :] = hi.astype(F32)
        fl_ref[j * 8 : j * 8 + 8, :] = lo.astype(F32)

    mine = lanes((PLANES, 128)) % 16 == sublanes((PLANES, 128))
    w = w_ref[...]

    def carry(f, shift):
        parts = [[ret_ref[pl.ds((16 * h + 8 * q) * 12 + f + shift, 8, stride=12), :] for h in range(2)] for q in range(2)]
        return jnp.concatenate([jnp.concatenate(p, 1) for p in parts], 0)

    def planes(ref, j, f):
        v = ref[pl.ds(j * 8 + f, 8, stride=0), :]
        return jnp.where(mine, jnp.concatenate([v, v], 0), 0.0).astype(BF16)

    for f in range(FIELDS):
        in_ref[f] = carry(f, 0)
    run = [carry(f, 5) for f in range(FIELDS)]
    copies = []
    for t in reversed(range(4)):
        for j in reversed(range(8 * t, 8 * t + 8)):
            for f in range(FIELDS):
                scaled = base_ref[f, j * 16 : j * 16 + 16, :] + full(gain_ref, j, f) * in_ref[f]
                run[f] = scaled + full(low_ref, j, f) * run[f]
                sc_ref[f, j * 16 : j * 16 + 16, :] = run[f]
                hi, lo = halves(run[f] * full(sp_ref, j, f))
                at = f * 128 + (j % 8) * 16
                lhs_ref[t, at : at + 16, :] = jnp.concatenate([hi, lo, hi, planes(fe_ref, j, f), planes(fl_ref, j, f)], 1)
        out = jnp.dot(lhs_ref[t], w, preferred_element_type=F32)
        for f in range(FIELDS):
            for s in range(8):
                j, at = 8 * t + s, f * 128 + s * 16
                value = out[at : at + 16] + sc_ref[f, j * 16 : j * 16 + 16, :]
                for h in range(2):
                    res_ref[t, h, pl.ds(f * 128 + s, PLANES, stride=8), :] = value[:, 128 * h : 128 * h + 128]
        for h in range(2):
            source = res_ref.at[t, h].reshape(FIELDS * PLANES, 8, 128)
            copies.append(pltpu.make_async_copy(source, o_ref.at[:, t, h], sem.at[2 * t + h]))
            copies[-1].start()
    for copy in copies:
        copy.wait()


def params():
    return pltpu.CompilerParams(vmem_limit_bytes=24 * 1024 * 1024)


VM = pl.BlockSpec(memory_space=pltpu.VMEM)


def local(cotangent, lower, pivot, speed):
    stencil, edge = tables()
    sds = jax.ShapeDtypeStruct
    flat = cotangent.reshape(FIELDS, PLANES, 4, 8, 2, 128).transpose(0, 1, 2, 4, 3, 5)
    rows = sds((ROWS * 8 + 8, 128), F32)
    left, right, cells, rise, fall, gain, unit = pl.pallas_call(
        edge_kernel,
        out_shape=[sds((FIELDS, 8, 128), F32)] * 2 + [sds((FIELDS, 4, 2, PLANES, 8, 128), F32), rows, rows, rows, sds((2, 8, 128), F32)],
        in_specs=[pl.BlockSpec(memory_space=pltpu.HBM)] * 4,
        out_specs=[VM] * 7,
        scratch_shapes=[
            pltpu.VMEM((384, 128), BF16),
            pltpu.VMEM((FIELDS, ROWS), F32),
            pltpu.VMEM((FIELDS, ROWS), F32),
            pltpu.SemaphoreType.DMA((8 * FIELDS + 3,)),
        ],
        compiler_params=params(),
        name="edge",
    )(*[pltpu.with_memory_space_constraint(v, pltpu.HBM) for v in (flat, jnp.asarray(edge), lower, pivot)])
    cells = cells.reshape(FIELDS, 1024, 128)
    count = lax.axis_size("stream")
    from_left = lax.ppermute(right, "stream", [(i, (i + 1) % count) for i in range(count)])
    from_right = lax.ppermute(left, "stream", [((i + 1) % count, i) for i in range(count)])
    main, base, low, inv, sp = pl.pallas_call(
        sums_kernel,
        out_shape=[sds((WALLS * 16, 128), F32), sds((FIELDS, ROWS * PLANES, CELLS), F32), rows, rows, rows],
        in_specs=[VM] * 5,
        out_specs=[VM] * 5,
        compiler_params=params(),
        cost_estimate=pl.CostEstimate(flops=4000000, bytes_accessed=2600000, transcendentals=0),
        name="sums",
    )(cells, fall, lower, pivot, speed)
    send, ext = pl.pallas_call(
        merge_kernel,
        out_shape=[sds((WALLS, 16, 128), F32), rows],
        in_specs=[VM] * 6,
        out_specs=[VM] * 2,
        compiler_params=params(),
        name="merge",
    )(main, rise, fall, unit, from_left, from_right)
    got = lax.all_to_all(send, "wall", 0, 0, tiled=True)
    carries, seam = pl.pallas_call(
        carry_kernel,
        out_shape=[sds((WALLS * 12, 128), F32), sds((2, 8, 128), F32)],
        in_specs=[VM],
        out_specs=[VM] * 2,
        scratch_shapes=[pltpu.VMEM((WALLS, 8, 128), F32)] * 2,
        compiler_params=params(),
        name="carry",
    )(got)
    back = lax.all_to_all(carries.reshape(WALLS, 3, 4, 128), "wall", 0, 0, tiled=True)
    out = pl.pallas_call(
        final_kernel,
        out_shape=sds((FIELDS * PLANES, 4, 2, 8, 128), F32),
        in_specs=[VM] * 9,
        out_specs=pl.BlockSpec(memory_space=pl.ANY),
        scratch_shapes=[pltpu.VMEM((ROWS * 8 + 8, 128), F32)] * 2
        + [
            pltpu.VMEM((FIELDS, PLANES, CELLS), F32),
            pltpu.VMEM((FIELDS, ROWS * PLANES, CELLS), F32),
            pltpu.VMEM((4, FIELDS * PLANES * 8, 1024), BF16),
            pltpu.VMEM((4, 2, FIELDS * PLANES * 8, 128), F32),
            pltpu.SemaphoreType.DMA((8,)),
        ],
        compiler_params=params(),
        name="final",
    )(base, back.reshape(WALLS * 12, 128), seam, low, inv, gain, sp, ext, jnp.asarray(stencil))
    return out.reshape(FIELDS, PLANES, 4, 2, 8, 128).transpose(0, 1, 2, 4, 3, 5).reshape(FIELDS, PLANES, ROWS, CELLS)


def solution(mesh):
    return jax.shard_map(
        local,
        mesh=mesh,
        in_specs=(P(None, None, "wall", "stream"), P(None, "wall"), P(None, "wall"), P(None, "wall")),
        out_specs=P(None, None, "wall", "stream"),
        check_vma=False,
    )
```

```python
import math

import jax
import jax.numpy as jnp
import ml_dtypes
import numpy as np
from jax import lax
from jax.experimental import pallas as pl
from jax.experimental.pallas import tpu as pltpu
from jax.sharding import PartitionSpec as P

F32, BF16 = jnp.float32, jnp.bfloat16
R = (math.sqrt(5.0) - 3.0) / 2.0
GAIN = 3.0 / math.sqrt(5.0)
C1 = 7.0 / 9.0
C2 = 1.0 / 36.0
FIELDS, PLANES, ROWS, CELLS, WALLS = 5, 16, 32, 256, 32


def split_np(w):
    w = np.asarray(w, np.float64)
    hi = w.astype(ml_dtypes.bfloat16)
    lo = (w - hi.astype(np.float64)).astype(ml_dtypes.bfloat16)
    return hi, lo


def tables():
    dec = lambda n: np.where(np.abs(n) % 2 == 0, 1.0, -1.0) * np.abs(R) ** np.abs(n)
    off = np.arange(CELLS)[:, None] - np.arange(CELLS)[None, :]
    tap = lambda o: GAIN * (C1 * (dec(o - 1) - dec(o + 1)) + C2 * (dec(o - 2) - dec(o + 2)))
    whi, wlo = split_np(tap(off))
    kappa = GAIN * (C1 * (1.0 / R - R) + C2 * (R**-2 - R**2))
    corr = tap(np.array(-1)) + kappa * R
    x = np.arange(CELLS)
    ext = np.zeros((4, CELLS))
    ext[0] = kappa * dec(CELLS - x)
    ext[1, CELLS - 1] = -corr
    ext[2] = -kappa * dec(x + 1)
    ext[3, 0] = corr
    ehi, elo = split_np(np.repeat(ext, PLANES, axis=0))
    zero = np.zeros_like(elo)
    stencil = np.concatenate([whi, whi, wlo, ehi, elo, ehi, zero], axis=0)
    edge = np.zeros((CELLS, 4))
    edge[:, 0] = dec(x)
    edge[0, 1] = 1.0
    edge[:, 2] = dec(CELLS - 1 - x)
    edge[CELLS - 1, 3] = 1.0
    edge = np.concatenate([edge[:64], edge[CELLS - 64 :]], axis=0)
    edge = np.concatenate([np.repeat(edge, PLANES, axis=1), np.zeros((128, 64))], axis=1)
    ghi, glo = split_np(edge)
    return stencil, np.concatenate([ghi, ghi, glo], axis=0)


def halves(x):
    hi = x.astype(BF16)
    return hi, (x - hi.astype(F32)).astype(BF16)


def lanes(shape):
    return lax.broadcasted_iota(jnp.int32, shape, len(shape) - 1)


def sublanes(shape):
    return lax.broadcasted_iota(jnp.int32, shape, len(shape) - 2)


def edge_kernel(c_hbm, w_hbm, lower_hbm, pivot_hbm, left_ref, right_ref, c_ref, rise_ref, fall_ref, gain_ref, unit_ref, w_ref, lower_ref, pivot_ref, sem):
    small = [
        pltpu.make_async_copy(a, b, sem.at[i])
        for i, (a, b) in enumerate([(lower_hbm, lower_ref), (pivot_hbm, pivot_ref), (w_hbm, w_ref)])
    ]
    big = [
        [
            pltpu.make_async_copy(c_hbm.at[f, :, t, h], c_ref.at[f, t, h], sem.at[3 + (f * 4 + t) * 2 + h])
            for t in range(4)
            for h in range(2)
        ]
        for f in range(FIELDS)
    ]
    for copy in [small[2]] + big[0] + big[1] + small[:2] + sum(big[2:], []):
        copy.start()
    small[2].wait()
    w = w_ref[...]
    plane, lane = lanes((8, 128)) % 16, lanes((8, 128)) // 32

    def edges(f):
        ends = [c_ref[f, :, h].reshape(PLANES * ROWS, 128) for h in range(2)]
        hi, lo = halves(jnp.where(lanes((PLANES * ROWS, 128)) < 64, ends[0], ends[1]))
        sums = jnp.dot(jnp.concatenate([hi, lo, hi], axis=1), w, preferred_element_type=F32)
        own = []
        for t in range(4):
            part = sums[t * 128 : t * 128 + 8]
            for p in range(1, PLANES):
                part = jnp.where(plane == p, sums[t * 128 + p * 8 : t * 128 + p * 8 + 8], part)
            own.append(part)
        left = own[0]
        right = pltpu.roll(own[0], 96, 1)
        for q in range(1, 4):
            part = own[q]
            left = jnp.where(lane == q, pltpu.roll(part, 32 * q, 1), left)
            right = jnp.where(lane == q, pltpu.roll(part, (32 * q + 96) % 128, 1) if q != 1 else part, right)
        left_ref[f] = left
        right_ref[f] = right

    for copy in big[0] + big[1]:
        copy.wait()
    edges(0)
    edges(1)
    for copy in small[:2] + sum(big[2:], []):
        copy.wait()
    weights(lower_ref, pivot_ref, rise_ref, fall_ref, gain_ref, unit_ref)
    for f in range(2, FIELDS):
        edges(f)


def load_row(ref, f, t, s):
    return jnp.concatenate([ref[f, pl.ds(t * 256 + h * 128 + s, PLANES, stride=8), :] for h in range(2)], 1)


def full(ref, j, f):
    v = ref[pl.ds(j * 8 + f, 8, stride=0), :]
    return jnp.concatenate([jnp.concatenate([v, v], 0)] * 2, 1)


def spread_rows(value, out_ref):
    for j in range(ROWS):
        out_ref[j * 8 : j * 8 + FIELDS, :] = jnp.broadcast_to(value[:, j : j + 1], (FIELDS, 128))


def weights(lower_ref, pivot_ref, rise_ref, fall_ref, gain_ref, unit_ref):
    low, piv = lower_ref[...], 1.0 / pivot_ref[...]
    wide = lambda v, j: jnp.broadcast_to(v[:, j : j + 1], (FIELDS, 128))
    entry = jnp.ones((FIELDS, 128), F32)
    direct, spread = [], jnp.zeros((FIELDS, 128), F32)
    for j in range(ROWS):
        direct.append(entry * wide(piv, j))
        gain_ref[j * 8 : j * 8 + FIELDS, :] = direct[j]
        spread = spread + entry * direct[j]
        entry = entry * wide(low, j)
    leave, first = None, None
    for j in reversed(range(ROWS)):
        l = wide(low, j)
        leave = l if leave is None else l * leave
        first = direct[j] if first is None else direct[j] + l * first
        rise_ref[j * 8 : j * 8 + FIELDS, :] = leave
        fall_ref[j * 8 : j * 8 + FIELDS, :] = first
    unit_ref[0, :FIELDS, :] = entry
    unit_ref[1, :FIELDS, :] = spread


def sums_kernel(c_ref, fall_ref, lower_ref, pivot_ref, speed_ref, out_ref, base_ref, low_ref, inv_ref, sp_ref):
    spread_rows(lower_ref[...], low_ref)
    spread_rows(1.0 / pivot_ref[...], inv_ref)
    spread_rows(speed_ref[...], sp_ref)
    for f in range(FIELDS):
        run = jnp.zeros((PLANES, CELLS), F32)
        down = jnp.zeros((PLANES, CELLS), F32)
        for j in range(ROWS):
            v = load_row(c_ref, f, j // 8, j % 8)
            down = down + full(fall_ref, j, f) * v
            run = v + run
            base_ref[f, j * 16 : j * 16 + 16, :] = run * full(inv_ref, j, f)
            run = run * full(low_ref, j, f)
        for h in range(2):
            for q in range(2):
                base = (16 * h + 8 * q) * 12 + f
                out_ref[pl.ds(base, 8, stride=12), :] = run[8 * q : 8 * q + 8, 128 * h : 128 * h + 128]
                out_ref[pl.ds(base + 5, 8, stride=12), :] = down[8 * q : 8 * q + 8, 128 * h : 128 * h + 128]


def merge_kernel(main_ref, rise_ref, fall_ref, unit_ref, left_ref, right_ref, out_ref, ext_ref):
    lane = lanes((8, 128))
    ups, downs = [], []
    for f in range(FIELDS):
        up = jnp.zeros((8, 128), F32)
        down = jnp.zeros((8, 128), F32)
        from_left, from_right = left_ref[f], right_ref[f]
        for q in range(4):
            r = pltpu.roll(from_right, (128 - 32 * q) % 128, 1) if q else from_right
            l = pltpu.roll(from_left, (128 - 32 * q + 32) % 128, 1) if q != 1 else from_left
            v = jnp.where(lane < 32, r, l)
            v = jnp.where(lane < 64, v, pltpu.roll(v, 64, 1))
            ext_ref[pl.ds(64 * q + f, 8, stride=8), :] = v
            up = up + rise_ref[pl.ds(64 * q + f, 8, stride=8), :] * v
            down = down + fall_ref[pl.ds(64 * q + f, 8, stride=8), :] * v
        ups.append(jnp.sum(up, axis=0, keepdims=True))
        downs.append(jnp.sum(down, axis=0, keepdims=True))
    row, lane5, lane1 = sublanes((FIELDS, 128)), lanes((FIELDS, 128)), lanes((1, 128))
    out_ref[...] = main_ref[...]
    for i, v in enumerate([ups, downs]):
        gains = jnp.sum(jnp.where(lane5 == 96 + row, unit_ref[i, :FIELDS, :], 0.0), axis=0, keepdims=True)
        for e in range(4):
            tail = gains
            for f in range(FIELDS):
                shift = (16 * f - 16 * e) % 128
                tail = jnp.where(lane1 // 16 == f, pltpu.roll(v[f], shift, 1) if shift else v[f], tail)
            out_ref[pl.ds(12 * e + 10 + i, 8, stride=48), :] = jnp.broadcast_to(tail, (8, 128))


def carry_kernel(in_ref, out_ref, through_ref, crest_ref):
    sub, lane = sublanes((8, 128)), lanes((8, 128))

    def gains(row):
        column = jnp.sum(jnp.where((lane == 96 + sub) & (sub < FIELDS), row, 0.0), axis=1, keepdims=True)
        spread = jnp.sum(jnp.where(lane // 16 == sub, column, 0.0), axis=0, keepdims=True)
        return jnp.where(sub < FIELDS, column, spread)

    run = jnp.zeros((8, 128), F32)
    for d in range(WALLS):
        at = 12 * d
        up, down = in_ref[at + 10 : at + 11, :], in_ref[at + 11 : at + 12, :]
        up, down = jnp.broadcast_to(up, (8, 128)), jnp.broadcast_to(down, (8, 128))
        through = gains(up)
        through_ref[d] = through
        out_ref[at : at + 5, :] = run[:5]
        out_ref[at + 10 : at + 11, :] = run[5:6]
        if d < WALLS - 1:
            last = in_ref[at + 5 : at + 13, :]
        else:
            last = pltpu.roll(in_ref[at + 4 : at + 12, :], 7, 0)
        crest_ref[d] = jnp.where(sub < FIELDS, last, down) + gains(down) * run
        run = through * run + jnp.where(sub < FIELDS, in_ref[at : at + 8, :], up)
    run = jnp.zeros((8, 128), F32)
    for d in reversed(range(WALLS)):
        at = 12 * d
        out_ref[at + 5 : at + 10, :] = run[:5]
        out_ref[at + 11 : at + 12, :] = run[5:6]
        run = through_ref[d] * run + crest_ref[d]


def final_kernel(
    base_ref, ret_ref, low_ref, inv_ref, gain_ref, sp_ref, ext_ref, w_ref, o_ref, fe_ref, fl_ref, in_ref, sc_ref, lhs_ref, res_ref, sem
):
    sub, lane = sublanes((8, 128)), lanes((8, 128))

    def unpack(i):
        out = jnp.zeros((8, 128), F32)
        for e in range(4):
            row = ret_ref[12 * e + 10 + i : 12 * e + 11 + i, :]
            for f in range(FIELDS):
                shift = (16 * e - 16 * f) % 128
                moved = pltpu.roll(row, shift, 1) if shift else row
                out = jnp.where((sub == f) & (lane // 16 == e), moved, out)
        return jnp.where(lane < 64, out, pltpu.roll(out, 64, 1))

    run = unpack(0)
    for j in range(ROWS):
        run = ext_ref[j * 8 : j * 8 + 8, :] + run
        fe_ref[j * 8 : j * 8 + 8, :] = run * inv_ref[j * 8 : j * 8 + 8, :]
        run = run * low_ref[j * 8 : j * 8 + 8, :]
    run = unpack(1)
    for j in reversed(range(ROWS)):
        run = fe_ref[j * 8 : j * 8 + 8, :] + low_ref[j * 8 : j * 8 + 8, :] * run
        fe_ref[j * 8 : j * 8 + 8, :] = run * sp_ref[j * 8 : j * 8 + 8, :]

    for j in range(ROWS):
        hi, lo = halves(fe_ref[j * 8 : j * 8 + 8, :])
        fe_ref[j * 8 : j * 8 + 8, :] = hi.astype(F32)
        fl_ref[j * 8 : j * 8 + 8, :] = lo.astype(F32)

    mine = lanes((PLANES, 128)) % 16 == sublanes((PLANES, 128))
    w = w_ref[...]

    def carry(f, shift):
        parts = [[ret_ref[pl.ds((16 * h + 8 * q) * 12 + f + shift, 8, stride=12), :] for h in range(2)] for q in range(2)]
        return jnp.concatenate([jnp.concatenate(p, 1) for p in parts], 0)

    def planes(ref, j, f):
        v = ref[pl.ds(j * 8 + f, 8, stride=0), :]
        return jnp.where(mine, jnp.concatenate([v, v], 0), 0.0).astype(BF16)

    for f in range(FIELDS):
        in_ref[f] = carry(f, 0)
    run = [carry(f, 5) for f in range(FIELDS)]
    copies = []
    for t in reversed(range(4)):
        for j in reversed(range(8 * t, 8 * t + 8)):
            for f in range(FIELDS):
                scaled = base_ref[f, j * 16 : j * 16 + 16, :] + full(gain_ref, j, f) * in_ref[f]
                run[f] = scaled + full(low_ref, j, f) * run[f]
                sc_ref[f, j * 16 : j * 16 + 16, :] = run[f]
                hi, lo = halves(run[f] * full(sp_ref, j, f))
                at = f * 128 + (j % 8) * 16
                lhs_ref[t, at : at + 16, :] = jnp.concatenate([hi, lo, hi, planes(fe_ref, j, f), planes(fl_ref, j, f)], 1)
        out = jnp.dot(lhs_ref[t], w, preferred_element_type=F32)
        for f in range(FIELDS):
            for s in range(8):
                j, at = 8 * t + s, f * 128 + s * 16
                value = out[at : at + 16] + sc_ref[f, j * 16 : j * 16 + 16, :]
                for h in range(2):
                    res_ref[t, h, pl.ds(f * 128 + s, PLANES, stride=8), :] = value[:, 128 * h : 128 * h + 128]
        for h in range(2):
            source = res_ref.at[t, h].reshape(FIELDS * PLANES, 8, 128)
            copies.append(pltpu.make_async_copy(source, o_ref.at[:, t, h], sem.at[2 * t + h]))
            copies[-1].start()
    for copy in copies:
        copy.wait()


def params():
    return pltpu.CompilerParams(vmem_limit_bytes=24 * 1024 * 1024)


VM = pl.BlockSpec(memory_space=pltpu.VMEM)


def local(cotangent, lower, pivot, speed):
    stencil, edge = tables()
    sds = jax.ShapeDtypeStruct
    flat = cotangent.reshape(FIELDS, PLANES, 4, 8, 2, 128).transpose(0, 1, 2, 4, 3, 5)
    rows = sds((ROWS * 8 + 8, 128), F32)
    left, right, cells, rise, fall, gain, unit = pl.pallas_call(
        edge_kernel,
        out_shape=[sds((FIELDS, 8, 128), F32)] * 2 + [sds((FIELDS, 4, 2, PLANES, 8, 128), F32), rows, rows, rows, sds((2, 8, 128), F32)],
        in_specs=[pl.BlockSpec(memory_space=pltpu.HBM)] * 4,
        out_specs=[VM] * 7,
        scratch_shapes=[
            pltpu.VMEM((384, 128), BF16),
            pltpu.VMEM((FIELDS, ROWS), F32),
            pltpu.VMEM((FIELDS, ROWS), F32),
            pltpu.SemaphoreType.DMA((8 * FIELDS + 3,)),
        ],
        compiler_params=params(),
        name="edge",
    )(*[pltpu.with_memory_space_constraint(v, pltpu.HBM) for v in (flat, jnp.asarray(edge), lower, pivot)])
    cells = cells.reshape(FIELDS, 1024, 128)
    count = lax.axis_size("stream")
    from_left = lax.ppermute(right, "stream", [(i, (i + 1) % count) for i in range(count)])
    from_right = lax.ppermute(left, "stream", [((i + 1) % count, i) for i in range(count)])
    main, base, low, inv, sp = pl.pallas_call(
        sums_kernel,
        out_shape=[sds((WALLS * 12, 128), F32), sds((FIELDS, ROWS * PLANES, CELLS), F32), rows, rows, rows],
        in_specs=[VM] * 5,
        out_specs=[VM] * 5,
        compiler_params=params(),
        cost_estimate=pl.CostEstimate(flops=4000000, bytes_accessed=2600000, transcendentals=0),
        name="sums",
    )(cells, fall, lower, pivot, speed)
    send, ext = pl.pallas_call(
        merge_kernel,
        out_shape=[sds((WALLS * 12, 128), F32), rows],
        in_specs=[VM] * 6,
        out_specs=[VM] * 2,
        compiler_params=params(),
        name="merge",
    )(main, rise, fall, unit, from_left, from_right)
    got = lax.all_to_all(send.reshape(WALLS, 3, 4, 128), "wall", 0, 0, tiled=True)
    carries = pl.pallas_call(
        carry_kernel,
        out_shape=sds((WALLS * 12, 128), F32),
        in_specs=[VM],
        out_specs=VM,
        scratch_shapes=[pltpu.VMEM((WALLS, 8, 128), F32)] * 2,
        compiler_params=params(),
        name="carry",
    )(got.reshape(WALLS * 12, 128))
    back = lax.all_to_all(carries.reshape(WALLS, 3, 4, 128), "wall", 0, 0, tiled=True)
    out = pl.pallas_call(
        final_kernel,
        out_shape=sds((FIELDS * PLANES, 4, 2, 8, 128), F32),
        in_specs=[VM] * 8,
        out_specs=pl.BlockSpec(memory_space=pl.ANY),
        scratch_shapes=[pltpu.VMEM((ROWS * 8 + 8, 128), F32)] * 2
        + [
            pltpu.VMEM((FIELDS, PLANES, CELLS), F32),
            pltpu.VMEM((FIELDS, ROWS * PLANES, CELLS), F32),
            pltpu.VMEM((4, FIELDS * PLANES * 8, 1024), BF16),
            pltpu.VMEM((4, 2, FIELDS * PLANES * 8, 128), F32),
            pltpu.SemaphoreType.DMA((8,)),
        ],
        compiler_params=params(),
        name="final",
    )(base, back.reshape(WALLS * 12, 128), low, inv, gain, sp, ext, jnp.asarray(stencil))
    return out.reshape(FIELDS, PLANES, 4, 2, 8, 128).transpose(0, 1, 2, 4, 3, 5).reshape(FIELDS, PLANES, ROWS, CELLS)


def solution(mesh):
    return jax.shard_map(
        local,
        mesh=mesh,
        in_specs=(P(None, None, "wall", "stream"), P(None, "wall"), P(None, "wall"), P(None, "wall")),
        out_specs=P(None, None, "wall", "stream"),
        check_vma=False,
    )
```
